512 devices in a mesh: tm: 8 (over y, core), chan: 64 (over z, x).
Axes of the slice: x: 4, y: 4, z: 16, core: 2. Of those that a mesh axis runs over, the one named last changes fastest.
Arguments:
- spectra: bfloat16 [8, 8192, 8192], P('tm', 'chan'), may hold values from -6 to 6
- block_counts: int32 [64], replicated, may hold values from 1 to 128, 6144 in all
- pairs: int32 [96, 3], replicated, may hold values from 0 to 63, as said below
Outputs:
- stacks: float32 [192, 128, 1024], P('chan', 'tm')
The draws below stay inside these ranges and needn't reach their ends.
Inputs may be any that keep to these rules, and one draw needn't show every extreme that they name: `pairs`: each owner holds at most 3 pair blocks and some owner holds exactly 3; all pair blocks of one owner share their source block; a target block never equals its source block.
All inputs are finite; a program needn't handle non-finite values.
Results may differ from the reference program's by a relative error of at most 0.0049.
Values may be sent and summed in bfloat16 or wider, within the bound.
A program may use at most 128 MiB of HBM per device.

```python
import math
import jax
import jax.numpy as jnp
import numpy as np
from jax import lax

F = 4096
BAND = 64
BLK = 128
LAGS = 8
SLOTS = 3
SEGMENTS = 8
NBLK = 64
CHANNELS = 8192
NPAIRS = 96


def draw_pairs(key, part):
    keys = jax.random.split(key, 6)
    total = NBLK * SLOTS
    order = jax.random.permutation(keys[0], total).astype(jnp.int32)
    busiest = jax.random.randint(keys[1], (), 0, NBLK)
    positions = jnp.arange(total, dtype=jnp.int32)
    score = order + jnp.where(positions // SLOTS == busiest, -total, 0)
    chosen = jnp.argsort(score, stable=True)[:NPAIRS].astype(jnp.int32)
    chosen = chosen[jax.random.permutation(keys[5], NPAIRS)]
    owners = chosen // SLOTS
    source_of = jax.random.randint(keys[2], (NBLK,), 0, NBLK)
    sources = source_of[owners]
    offsets = jax.random.randint(keys[3], (NPAIRS,), 1, NBLK)
    forced = 1 + chosen % SLOTS + SLOTS * jax.random.randint(keys[4], (NPAIRS,), 0, (NBLK - 1) // SLOTS)
    offsets = jnp.where(owners == busiest, forced, offsets)
    targets = jnp.mod(sources + offsets, NBLK)
    return jnp.stack([sources, targets, owners], axis=1).astype(jnp.int32)


def steps_of(rng, extent, cuts, low, top_value):
    loudness = 1.0
    for position, shards_of in cuts:
        draws = jax.random.uniform(jax.random.fold_in(jax.random.fold_in(rng, 6), position), (shards_of,), jnp.float32, low / len(cuts), top_value / len(cuts))
        loudness = loudness * jnp.repeat(jnp.exp(draws), extent[position] // shards_of).reshape((-1,) + (1,) * (len(extent) - 1 - position))
    return loudness


def split_up(count, total, reach, lean):
    loads = [(1 << 20) // math.isqrt(standing ** lean) + 1 for standing in range(2, count + 1)]
    rest, holding = total - reach - (count - 1), [1] * (count - 1)
    while rest > 0:
        movable = [i for i in range(count - 1) if holding[i] < reach]
        whole, remaining = sum([loads[i] for i in movable]), rest
        for i in movable:
            extra = min(reach - holding[i], max(1, remaining * loads[i] // whole), rest)
            holding[i] = holding[i] + extra
            rest = rest - extra
    return np.array([reach] + holding)


def ragged(rng, number_of, total, most, slope):
    if number_of == 2:
        one = jax.random.randint(rng, (), max(1, total - most), min(most, total - 1) + 1)
        return jnp.stack([one, total - one])
    sizes = jnp.asarray(split_up(number_of, total, most, slope), jnp.int32)
    couples = (number_of - 1) // 2
    giver, receiver = sizes[1:1 + 2 * couples:2], sizes[2:2 + 2 * couples:2]
    margin = jnp.minimum(giver - 1, most - receiver)
    moved = jax.random.randint(jax.random.fold_in(rng, 1), (couples,), 0, 1 << 20) % (margin + 1)
    sizes = sizes.at[1:1 + 2 * couples:2].set(giver - moved).at[2:2 + 2 * couples:2].set(receiver + moved)
    return sizes[jax.random.permutation(jax.random.fold_in(rng, 2), number_of)]


def gaussian(own_key, extent, scale, most, cuts=(), held_as=jnp.bfloat16):
    drawn = scale * jax.random.normal(own_key, extent, jnp.float32)
    if cuts:
        drawn = drawn * steps_of(own_key, extent, cuts, -0.22, 0.18)
    return jnp.clip(drawn, -most, most).astype(held_as)


def setup_inputs(seed: int = 0) -> dict:
    arg_keys = jax.random.split(jax.random.key(seed), 4)
    spectra = gaussian(arg_keys[0], (SEGMENTS, CHANNELS, 2 * F), 1.0, 6.0, ((0, 8), (1, 64)))
    block_counts = ragged(arg_keys[1], NBLK, NBLK * (BLK - BLK // 4), BLK, 1).astype(jnp.int32)
    pairs = draw_pairs(jax.random.fold_in(arg_keys[3], 71), 0)
    return {"spectra": spectra, "block_counts": block_counts, "pairs": pairs}


def phase_tables():
    freq_index = jnp.arange(F // BAND, dtype=jnp.int32)[:, None] * BAND + jnp.arange(BAND, dtype=jnp.int32)[None, :]
    lag_values = jnp.arange(LAGS, dtype=jnp.int32) - LAGS // 2
    phase = jnp.mod(lag_values[:, None, None] * freq_index[None], 2 * F)
    angle = jnp.pi * phase.astype(jnp.float32) / F
    return (jnp.cos(angle), jnp.sin(angle))

def whiten(raw, live_count):
    segs, rows, width = raw.shape
    values = raw.astype(jnp.float32).reshape(segs, rows, width // (2 * BAND), 2, BAND)
    power = lax.optimization_barrier(jnp.mean(values[..., 0, :] ** 2 + values[..., 1, :] ** 2, axis=-1))
    alive = (jnp.arange(rows, dtype=jnp.int32) < live_count).astype(jnp.float32)
    scaled = values * lax.rsqrt(power + 1e-06)[..., None, None] * alive[None, :, None, None, None]
    return scaled.astype(jnp.bfloat16).reshape(segs, rows, width)

def pair_ranks(pairs):
    owners = pairs[:, 2]
    places = jnp.arange(pairs.shape[0], dtype=jnp.int32)
    same_owner = (owners[:, None] == owners[None, :]) & (places[None, :] < places[:, None])
    return lax.optimization_barrier(jnp.sum(same_owner.astype(jnp.int32), axis=1)).astype(jnp.int32)

def correlate(source, target, cosine, sine, scale):
    segs, rows, width = source.shape
    bands = width // (2 * BAND)
    src = source.reshape(segs, rows, bands, 2, BAND).astype(jnp.float32)
    tgt = target.reshape(segs, rows, bands, 2, BAND).astype(jnp.float32)
    real_part = tgt[..., 0, :][:, None]
    imag_part = tgt[..., 1, :][:, None]
    cos_b = cosine[None, :, None]
    sin_b = sine[None, :, None]
    mod_real = real_part * cos_b + imag_part * sin_b
    mod_imag = imag_part * cos_b - real_part * sin_b
    moved = jnp.stack([mod_real, mod_imag], axis=-2).astype(jnp.bfloat16).astype(jnp.float32)
    corr = jnp.einsum('siqpf,smjqpf->imj', src, moved)
    return (corr * scale).reshape(rows, LAGS * rows)

def reference(spectra, block_counts, pairs):
    cosine, sine = phase_tables()
    ranks = pair_ranks(pairs)
    scale = 1.0 / math.sqrt(2.0 * F * SEGMENTS)

    def block_of(block_id):
        raw = lax.dynamic_slice_in_dim(spectra, (block_id * BLK).astype(jnp.int32), BLK, 1)
        return whiten(raw, block_counts[block_id])

    def one_pair(stacks, row):
        corr = correlate(block_of(row[0]), block_of(row[1]), cosine, sine, scale)
        target_row = (row[2] * SLOTS + row[3]).astype(jnp.int32)
        zero_index = jnp.zeros((), jnp.int32)
        stacks = lax.dynamic_update_slice(stacks, corr[None], (target_row, zero_index, zero_index))
        return (stacks, None)
    rows_all = jnp.concatenate([pairs, ranks[:, None]], axis=1).astype(jnp.int32)
    initial = jnp.zeros((NBLK * SLOTS, BLK, LAGS * BLK), jnp.float32)
    return lax.scan(one_pair, initial, rows_all)[0]
```

```python
import functools

import jax
import jax.numpy as jnp
from jax import lax
from jax.experimental import pallas as pl
from jax.experimental.pallas import tpu as pltpu
from jax.sharding import PartitionSpec as P

F = 4096
BAND = 64
BLK = 128
LAGS = 8
SLOTS = 3
NBLK = 64
NPAIRS = 96
SCALE = 1.0 / 256.0
MESH = pl.DeviceIdType.MESH

NZ, NX, NY = 16, 4, 4
BANDS = F // BAND // NZ
WIDE = 2 * BAND
HALF = 12
MINE = 2 * HALF
BF16 = jnp.bfloat16
F32 = jnp.float32


def place():
    tm, chan = lax.axis_index("tm"), lax.axis_index("chan")
    return tm // 2, tm % 2, chan // NX, chan % NX


def remote(src, dst, send, recv, where):
    return pltpu.make_async_remote_copy(
        src_ref=src, dst_ref=dst, send_sem=send, recv_sem=recv, device_id=where, device_id_type=MESH
    )


def signal_all(barrier, wheres):
    for where in wheres:
        pl.semaphore_signal(barrier, inc=1, device_id=where, device_id_type=MESH)
    pl.semaphore_wait(barrier, len(wheres))


def spread(spec, held, zsend, zrecv, xsend, xrecv, local):
    _, _, z, x = place()
    right = {"chan": z * NX + (x + 1) % NX}
    left = {"chan": z * NX + (x + NX - 1) % NX}
    xl, xr = (x + NX - 1) % NX, (x + 1) % NX

    order = [NZ // 2] + [d for k in range(NZ // 2 - 1, 0, -1) for d in (k, NZ - k)]
    signal_all(
        pltpu.get_barrier_semaphore(),
        [{"chan": (z + d) % NZ * NX + x} for d in range(1, NZ)] + [left, right],
    )

    def columns(zt, q):
        return spec.at[0, :, pl.ds(pl.multiple_of((zt * BANDS + q) * WIDE, WIDE), WIDE)]

    for q in range(BANDS):
        for d in order:
            zt = (z + d) % NZ
            remote(
                columns(zt, q), held.at[q, x, z], zsend.at[q], zrecv.at[q], {"chan": zt * NX + x}
            ).start()
        pltpu.make_async_copy(columns(z, q), held.at[q, x, z], local.at[q]).start()

    rest = NZ - 1
    half = NZ // 2

    def xcopies(q):
        own = held.at[q, x]
        return (remote(own, own, xsend.at[q, 0], xrecv.at[q, 0], right),
                remote(own, own, xsend.at[q, 1], xrecv.at[q, 1], left))

    def fcopies(q):
        lo = held.at[q, xl, pl.ds(0, half)]
        hi = held.at[q, xr, pl.ds(half, half)]
        return (remote(lo, lo, xsend.at[q, 2], xrecv.at[q, 2], right),
                remote(hi, hi, xsend.at[q, 3], xrecv.at[q, 3], left))

    def forward(q):
        a, b = xcopies(q)
        a.wait_recv()
        fcopies(q)[0].start()
        b.wait_recv()
        fcopies(q)[1].start()

    for q in range(BANDS):
        pltpu.make_async_copy(columns(z, q), held.at[q, x, z], local.at[q]).wait()
        got = held.at[q, x, pl.ds(0, rest)]
        pltpu.make_async_copy(got, got, zrecv.at[q]).wait()
        for c in xcopies(q):
            c.start()
        if q:
            forward(q - 1)
    forward(BANDS - 1)
    for q in range(BANDS):
        got = held.at[q, x, pl.ds(0, rest)]
        pltpu.make_async_copy(got, got, zsend.at[q]).wait()
        for c in xcopies(q):
            c.wait_send()
        for c in fcopies(q):
            c.wait_send()
            c.wait_recv()


def call_spread(spectra):
    return pl.pallas_call(
        spread,
        out_shape=jax.ShapeDtypeStruct((BANDS, NX, NZ, BLK, WIDE), BF16),
        in_specs=[pl.BlockSpec(memory_space=pltpu.VMEM)],
        out_specs=pl.BlockSpec(memory_space=pl.ANY),
        scratch_shapes=[
            pltpu.SemaphoreType.DMA((BANDS,)),
            pltpu.SemaphoreType.DMA((BANDS,)),
            pltpu.SemaphoreType.DMA((BANDS, 4)),
            pltpu.SemaphoreType.DMA((BANDS, 4)),
            pltpu.SemaphoreType.DMA((BANDS,)),
        ],
        compiler_params=pltpu.CompilerParams(collective_id=0, has_side_effects=True),
        name="spread",
    )(spectra)


def correlate(table, counts, held, cosine, sine, out, white, moved):
    step = pl.program_id(0)

    @pl.when(step == 0)
    def _():
        lane_row = lax.broadcasted_iota(jnp.int32, (BLK, WIDE), 0)

        def one(zs, carry):
            for xs in range(NX):
                alive = (lane_row < counts[zs * NX + xs]).astype(F32)
                for q in range(BANDS):
                    v = held[q, xs, zs].astype(F32)
                    power = jnp.sum(v * v, axis=-1, keepdims=True) * (1.0 / BAND)
                    scaled = v * lax.rsqrt(power + 1e-06) * alive
                    white[zs * NX + xs, :, q * WIDE : (q + 1) * WIDE] = scaled.astype(BF16)
            return carry

        lax.fori_loop(0, NZ, one, 0)

    source, target = table[0, step], table[1, step]
    for q in range(BANDS):
        cols = slice(q * WIDE, (q + 1) * WIDE)
        v = white[target, :, cols].astype(F32)
        w = pltpu.roll(v, BAND, 1)
        for m in range(LAGS):
            c = cosine[q, m : m + 1, :]
            s = sine[q, m : m + 1, :]
            moved[m * BLK : (m + 1) * BLK, cols] = (v * c + w * s).astype(BF16)
    corr = lax.dot_general(
        white[source], moved[...], (((1,), (1,)), ((), ())), preferred_element_type=F32
    )
    out[0] = (corr * SCALE).astype(BF16)


def call_correlate(table, counts, held, cosine, sine):
    whole = lambda *_: (0,) * 5
    return pl.pallas_call(
        correlate,
        out_shape=jax.ShapeDtypeStruct((MINE, BLK, LAGS * BLK), BF16),
        grid_spec=pltpu.PrefetchScalarGridSpec(
            num_scalar_prefetch=2,
            grid=(MINE,),
            in_specs=[
                pl.BlockSpec((BANDS, NX, NZ, BLK, WIDE), whole, pipeline_mode=pl.Buffered(1)),
                pl.BlockSpec((BANDS, LAGS, WIDE), lambda *_: (0, 0, 0)),
                pl.BlockSpec((BANDS, LAGS, WIDE), lambda *_: (0, 0, 0)),
            ],
            out_specs=pl.BlockSpec((1, BLK, LAGS * BLK), lambda i, *_: (i, 0, 0)),
            scratch_shapes=[
                pltpu.VMEM((NBLK, BLK, BANDS * WIDE), BF16),
                pltpu.VMEM((LAGS * BLK, BANDS * WIDE), BF16),
            ],
        ),
        compiler_params=pltpu.CompilerParams(vmem_limit_bytes=48 << 20),
        name="correlate",
    )(table, counts, held, cosine, sine)


ROWS = 16
TILE = 128
SUB = 2
SUBN = HALF // SUB


def collect(
    part, sends, takes, out,
    mine, other, h, u, v, sums, cp, cm, final, give, got,
    lsem, csend, crecv, ysend, yrecv, psend, precv, msend, mrecv, gsend, grecv,
):
    y, c, z, x = place()
    tm, chan = lax.axis_index("tm"), lax.axis_index("chan")
    core = {"tm": y * 2 + 1 - c}
    up, down = {"tm": (y + 1) % NY * 2 + c}, {"tm": (y + NY - 1) % NY * 2 + c}
    zup, zdown = {"chan": (z + 1) % NZ * NX + x}, {"chan": (z + NZ - 1) % NZ * NX + x}
    owners = NZ * NX

    barrier = pltpu.get_barrier_semaphore()
    for where in (core, up, down):
        pl.semaphore_signal(barrier, inc=1, device_id=where, device_id_type=MESH)

    def greet(d, carry):
        pl.semaphore_signal(
            barrier, inc=1, device_id={"chan": (chan + d) % owners}, device_id_type=MESH
        )
        return carry

    lax.fori_loop(1, owners, greet, 0)
    pl.semaphore_wait(barrier, owners + 2)

    turn = [(y + 2) % NY, (y + 1) % NY, (y + NY - 1) % NY, y]
    swaps = [
        remote(part.at[:, k, 1 - c], other.at[k], csend.at[i], crecv.at[i], core)
        for i, k in enumerate(turn)
    ]
    loads = [
        pltpu.make_async_copy(part.at[:, k, c], mine.at[k], lsem.at[i]) for i, k in enumerate(turn)
    ]
    for a, b in zip(swaps, loads):
        a.start()
        b.start()

    def add_swap(i):
        loads[i].wait()
        swaps[i].wait_recv()
        k = turn[i]

        def one(p, carry):
            mine[k, p] = (mine[k, p].astype(F32) + other[k, p].astype(F32)).astype(BF16)
            return carry

        lax.fori_loop(0, MINE, one, 0)

    lo, hi = pl.ds(0, HALF), pl.ds(HALF, HALF)
    y2, yp, ym = turn[0], turn[1], turn[2]
    ycopy = lambda i, src, dst, where: remote(src, dst, ysend.at[i], yrecv.at[i], where)
    far = [ycopy(0, mine.at[y2, lo], h.at[0], up), ycopy(1, mine.at[y2, hi], h.at[1], down)]
    raw = [ycopy(2, mine.at[yp, hi], u.at[0], up), ycopy(3, mine.at[ym, lo], v.at[0], down)]
    near = [ycopy(4, mine.at[yp, lo], u.at[1], up), ycopy(5, mine.at[ym, hi], v.at[1], down)]

    add_swap(0)
    far[0].start()
    far[1].start()
    add_swap(1)
    raw[0].start()
    add_swap(2)
    raw[1].start()
    add_swap(3)

    for i, (k, base) in enumerate(((yp, 0), (ym, HALF))):
        far[i].wait_recv()

        def one(p, carry):
            mine[k, base + p] = (
                mine[k, base + p].astype(F32) + h[i, p].astype(F32)
            ).astype(BF16)
            return carry

        lax.fori_loop(0, HALF, one, 0)
        near[i].start()

    raw[0].wait_recv()
    raw[1].wait_recv()
    near[0].wait_recv()
    near[1].wait_recv()
    for g in range(2):
        a, b = (u.at[1], v.at[0]) if g == 0 else (u.at[0], v.at[1])

        def one(p, carry):
            t = mine[y, g * HALF + p].astype(F32) + a[p].astype(F32) + b[p].astype(F32)
            for l in range(8):
                sums[g * 8 + l, p] = t[:, l * TILE : (l + 1) * TILE]
            return carry

        lax.fori_loop(0, HALF, one, 0)

    def hop(src, dst, send, recv, where):
        return remote(src, dst, send, recv, where)

    ups, downs = NZ // 2, NZ // 2 - 1
    start_up, start_down = (z + ups) % NZ, (z + NZ - downs) % NZ
    pieces = [pl.ds(b * SUBN, SUBN) for b in range(SUB)]

    def chain_up(s, b):
        src = sums.at[start_up, pieces[b]] if s == 0 else cp.at[s - 1, pieces[b]]
        return hop(src, cp.at[s, pieces[b]], psend.at[s, b], precv.at[s, b], zup)

    def chain_down(s, b):
        src = sums.at[start_down, pieces[b]] if s == 0 else cm.at[s - 1, pieces[b]]
        return hop(src, cm.at[s, pieces[b]], msend.at[s, b], mrecv.at[s, b], zdown)

    for b in range(SUB):
        chain_up(0, b).start()
        chain_down(0, b).start()
    for s in range(1, ups):
        for b in range(SUB):
            chain_up(s - 1, b).wait_recv()
            cp[s - 1, pieces[b]] = cp[s - 1, pieces[b]] + sums[(z + ups - s) % NZ, pieces[b]]
            chain_up(s, b).start()
            if s < downs:
                chain_down(s - 1, b).wait_recv()
                cm[s - 1, pieces[b]] = (
                    cm[s - 1, pieces[b]] + sums[(z + NZ - downs + s) % NZ, pieces[b]]
                )
                chain_down(s, b).start()
    for b in range(SUB):
        chain_down(downs - 1, b).wait_recv()
        chain_up(ups - 1, b).wait_recv()
    final[0:HALF] = (sums[z] + cp[ups - 1] + cm[downs - 1]).astype(BF16)
    final[HALF] = jnp.zeros((ROWS, TILE), BF16)

    def fill(o, carry):
        give[o] = final[sends[o]]
        return carry

    lax.fori_loop(0, owners, fill, 0)

    def deliver(d, carry):
        o = (chan + d) % owners
        remote(give.at[o], got.at[chan], gsend, grecv, {"chan": o}).start()
        return carry

    lax.fori_loop(1, owners, deliver, 0)
    got[chan] = give[chan]
    many = pl.ds(0, owners - 1)
    pltpu.make_async_copy(got.at[many], got.at[many], grecv).wait()

    for k in range(SLOTS):
        base, on = takes[0, k], takes[1, k]
        for l in range(8):
            t = got[base + l * NX].astype(F32)
            out[k, :, l * TILE : (l + 1) * TILE] = jnp.where(on > 0, t, 0.0)

    pltpu.make_async_copy(give.at[many], give.at[many], gsend).wait()
    for s in swaps:
        s.wait_send()
    for s in far + raw + near:
        s.wait_send()
    for b in range(SUB):
        for s in range(ups):
            chain_up(s, b).wait_send()
        for s in range(downs):
            chain_down(s, b).wait_send()


def call_collect(part, sends, takes):
    smem = pl.BlockSpec(memory_space=pltpu.SMEM)
    dma = pltpu.SemaphoreType.DMA
    side = (ROWS, LAGS * BLK)
    return pl.pallas_call(
        collect,
        out_shape=jax.ShapeDtypeStruct((SLOTS, ROWS, LAGS * BLK), F32),
        in_specs=[pl.BlockSpec(memory_space=pl.ANY), smem, smem],
        out_specs=pl.BlockSpec(memory_space=pltpu.VMEM),
        scratch_shapes=[
            pltpu.VMEM((NY, MINE, *side), BF16),
            pltpu.VMEM((NY, MINE, *side), BF16),
            pltpu.VMEM((2, HALF, *side), BF16),
            pltpu.VMEM((2, HALF, *side), BF16),
            pltpu.VMEM((2, HALF, *side), BF16),
            pltpu.VMEM((NZ, HALF, ROWS, TILE), F32),
            pltpu.VMEM((NZ // 2, HALF, ROWS, TILE), F32),
            pltpu.VMEM((NZ // 2 - 1, HALF, ROWS, TILE), F32),
            pltpu.VMEM((HALF + 1, ROWS, TILE), BF16),
            pltpu.VMEM((NBLK, ROWS, TILE), BF16),
            pltpu.VMEM((NBLK, ROWS, TILE), BF16),
            dma((NY,)), dma((NY,)), dma((NY,)),
            dma((6,)), dma((6,)),
            dma((NZ // 2, SUB)), dma((NZ // 2, SUB)),
            dma((NZ // 2 - 1, SUB)), dma((NZ // 2 - 1, SUB)),
            dma, dma,
        ],
        compiler_params=pltpu.CompilerParams(
            collective_id=1, has_side_effects=True, vmem_limit_bytes=40 << 20
        ),
        name="collect",
    )(part, sends, takes)


def phase_tables(z):
    band = z * BANDS + jnp.arange(BANDS, dtype=jnp.int32)
    freq = band[:, None, None] * BAND + jnp.arange(BAND, dtype=jnp.int32)[None, None, :]
    lag = jnp.arange(LAGS, dtype=jnp.int32)[None, :, None] - LAGS // 2
    phase = jnp.mod(lag * freq, 2 * F)
    angle = jnp.pi * phase.astype(F32) / F
    c, s = jnp.cos(angle), jnp.sin(angle)
    return jnp.concatenate([c, c], -1), jnp.concatenate([s, -s], -1)


def plans(pairs, chan):
    z, x = chan // NX, chan % NX
    owners = pairs[:, 2]
    places = jnp.arange(NPAIRS, dtype=jnp.int32)
    before = (owners[None, :] < owners[:, None]) | (
        (owners[None, :] == owners[:, None]) & (places[None, :] < places[:, None])
    )
    rank = jnp.sum(before.astype(jnp.int32), axis=1)
    wanted = places[:MINE] % HALF * 8 + places[:MINE] // HALF * 4 + x
    pick = (rank[None, :] == wanted[:, None]).astype(jnp.int32)
    table = jnp.sum(pick[None] * pairs.T[:2, None, :], axis=2)

    ids = jnp.arange(NBLK, dtype=jnp.int32)
    first = jnp.sum((owners[None, :] < ids[:, None]).astype(jnp.int32), axis=1)
    count = jnp.sum((owners[None, :] == ids[:, None]).astype(jnp.int32), axis=1)
    bin_ = z // 8 * 4 + x
    ahead = jnp.mod(bin_ - first, 8)
    sends = jnp.where(ahead < count, (first + ahead) // 8, HALF)

    me = (ids == chan).astype(jnp.int32)
    r = jnp.sum(me * first) + jnp.arange(SLOTS, dtype=jnp.int32)
    on = (jnp.arange(SLOTS, dtype=jnp.int32) < jnp.sum(me * count)).astype(jnp.int32)
    base = r % 8 // 4 * (8 * NX) + r % 4
    return table, sends, jnp.stack([base, on])


def per_device(spectra, block_counts, pairs):
    chan = lax.axis_index("chan")
    cosine, sine = phase_tables(chan // NX)
    table, sends, takes = plans(pairs, chan)
    held = call_spread(spectra)
    part = call_correlate(table, block_counts, held, cosine, sine)
    return call_collect(part.reshape(MINE, NY, 2, ROWS, LAGS * BLK), sends, takes)


def solution(mesh):
    placed = (P("tm", "chan", None), P(), P())
    return jax.shard_map(
        per_device, mesh=mesh, in_specs=placed, out_specs=P("chan", "tm", None), check_vma=False
    )
```

```python
import functools

import jax
import jax.numpy as jnp
from jax import lax
from jax.experimental import pallas as pl
from jax.experimental.pallas import tpu as pltpu
from jax.sharding import PartitionSpec as P

F = 4096
BAND = 64
BLK = 128
LAGS = 8
SLOTS = 3
NBLK = 64
NPAIRS = 96
SCALE = 1.0 / 256.0
MESH = pl.DeviceIdType.MESH

NZ, NX, NY = 16, 4, 4
BANDS = F // BAND // NZ
WIDE = 2 * BAND
HALF = 12
MINE = 2 * HALF
BF16 = jnp.bfloat16
F32 = jnp.float32


def place():
    tm, chan = lax.axis_index("tm"), lax.axis_index("chan")
    return tm // 2, tm % 2, chan // NX, chan % NX


def remote(src, dst, send, recv, where):
    return pltpu.make_async_remote_copy(
        src_ref=src, dst_ref=dst, send_sem=send, recv_sem=recv, device_id=where, device_id_type=MESH
    )


ROWS = 16
TILE = 128
PIECES = 2
PIECE = MINE // PIECES
SUBN = HALF // PIECES
GROUPS = ((0, 1, 15, 2), (14, 3, 13, 4), (12, 5, 11, 6), (10, 7, 9, 8))
RELAY = False


def kernel(
    spec, table, counts, cosine, sine, sends, takes, out,
    held, relay, white, moved, acc, part, mine, other, h, u, v, sums, cp, cm, final, give, got,
    local, zsend, zlow, zrecv, rsend, rrecv, rpass, xsend, xrecv, fsend, frecv,
    csend, crecv, ysend, yrecv, psend, precv, msend, mrecv, gsend, grecv,
):
    y, c, z, x = place()
    chan = lax.axis_index("chan")
    owners = NZ * NX
    xl, xr = (x + NX - 1) % NX, (x + 1) % NX
    right, left = {"chan": z * NX + xr}, {"chan": z * NX + xl}
    core = {"tm": y * 2 + 1 - c}
    up, down = {"tm": (y + 1) % NY * 2 + c}, {"tm": (y + NY - 1) % NY * 2 + c}
    zup, zdown = {"chan": (z + 1) % NZ * NX + x}, {"chan": (z + NZ - 1) % NZ * NX + x}

    barrier = pltpu.get_barrier_semaphore()
    for where in (core, up, down):
        pl.semaphore_signal(barrier, inc=1, device_id=where, device_id_type=MESH)

    def greet(d, carry):
        pl.semaphore_signal(
            barrier, inc=1, device_id={"chan": (chan + d) % owners}, device_id_type=MESH
        )
        return carry

    lax.fori_loop(1, owners, greet, 0)
    pl.semaphore_wait(barrier, owners + 2)

    def columns(zt, q, rows=slice(None)):
        return spec.at[0, rows, pl.ds(pl.multiple_of((zt * BANDS + q) * WIDE, WIDE), WIDE)]

    low, high = pl.ds(0, BLK // 2), pl.ds(BLK // 2, BLK // 2)

    def group_of(d):
        return [j for j, g in enumerate(GROUPS) if d in g][0]

    def own(q):
        return pltpu.make_async_copy(columns(z, q), held.at[q, x, z], local.at[q])

    def to_relay(q):
        return remote(columns((z + 8) % NZ, q, high), relay.at[q], rsend.at[q], rrecv.at[q], zdown)

    def from_relay(q):
        return remote(
            relay.at[q], held.at[q, x, (z + 1) % NZ, high], rpass.at[q], zrecv.at[q, 0],
            {"chan": (z + 9) % NZ * NX + x},
        )

    def zsends(q):
        for group in GROUPS:
            for d in group:
                zt = (z + d) % NZ
                where = {"chan": zt * NX + x}
                if d == 8 and RELAY:
                    remote(
                        columns(zt, q, low), held.at[q, x, z, low], zlow.at[q],
                        zrecv.at[q, 0], where,
                    ).start()
                elif d:
                    remote(
                        columns(zt, q), held.at[q, x, z], zsend.at[q],
                        zrecv.at[q, group_of(d)], where,
                    ).start()

    def zwait(q, j):
        n = len(GROUPS[j])
        if j == 0:
            own(q).wait()
            n -= 1
        got_ = held.at[q, x, pl.ds(0, n)]
        pltpu.make_async_copy(got_, got_, zrecv.at[q, j]).wait()

    def xstart(q, j):
        for d in GROUPS[j]:
            blk = held.at[q, x, (z + NZ - d) % NZ]
            remote(blk, blk, xsend.at[q, 0], xrecv.at[q, j, 0], right).start()
            remote(blk, blk, xsend.at[q, 1], xrecv.at[q, j, 1], left).start()

    def forward(q, j):
        n = len(GROUPS[j])
        for side, (xs, where) in enumerate(((xl, right), (xr, left))):
            got_ = held.at[q, xs, pl.ds(0, n)]
            pltpu.make_async_copy(got_, got_, xrecv.at[q, j, side]).wait()
            for d in GROUPS[j][side * 2 : side * 2 + 2]:
                blk = held.at[q, xs, (z + NZ - d) % NZ]
                remote(blk, blk, fsend.at[q, side], frecv.at[q, side], where).start()

    def fwait(q):
        got_ = held.at[q, x, pl.ds(0, NZ // 2)]
        for side in range(2):
            pltpu.make_async_copy(got_, got_, frecv.at[q, side]).wait()

    row = lax.broadcasted_iota(jnp.int32, (BLK, WIDE), 0)

    def whiten(q):
        def one(zs, carry):
            for xs in range(NX):
                b = zs * NX + xs
                alive = (row < counts[b]).astype(F32)
                t = held[q, xs, zs].astype(F32)
                power = jnp.sum(t * t, axis=-1, keepdims=True) * (1.0 / BAND)
                white[b] = (t * lax.rsqrt(power + 1e-06) * alive).astype(BF16)
            return carry

        lax.fori_loop(0, NZ, one, 0)

    def pair(q, p, slot):
        t = white[table[1, p]].astype(F32)
        w = pltpu.roll(t, BAND, 1)
        for m in range(LAGS):
            moved[slot, m * BLK : (m + 1) * BLK] = (
                t * cosine[q, m : m + 1, :] + w * sine[q, m : m + 1, :]
            ).astype(BF16)
        corr = lax.dot_general(
            white[table[0, p]], moved[slot], (((1,), (1,)), ((), ())), preferred_element_type=F32
        )
        if q == 0:
            acc[p] = corr
        elif q < BANDS - 1:
            acc[p] = acc[p] + corr
        else:
            total = ((acc[p] + corr) * SCALE).astype(BF16)
            for r in range(BLK // ROWS):
                part[p, r] = total[r * ROWS : (r + 1) * ROWS]

    def some_pairs(q, first, count):
        def one(i, carry):
            for slot in range(2):
                pair(q, first + i * 2 + slot, slot)
            return carry

        lax.fori_loop(0, count // 2, one, 0)

    if RELAY:
        for q in range(BANDS):
            to_relay(q).start()
    for q in range(BANDS):
        own(q).start()
        zsends(q)
        if RELAY:
            to_relay(q).wait_recv()
            from_relay(q).start()

    third = MINE // 3
    prev = None
    for q in range(BANDS):
        for j in range(len(GROUPS)):
            zwait(q, j)
            xstart(q, j)
            if prev is not None:
                forward(*prev)
            prev = (q, j)
            if q >= 1 and j == 1:
                fwait(q - 1)
                whiten(q - 1)
            elif q >= 1 and j >= 2:
                some_pairs(q - 1, (j - 2) * third, third)
            elif q >= 2 and j == 0:
                some_pairs(q - 2, 2 * third, third)
    forward(*prev)
    some_pairs(BANDS - 2, 2 * third, third)
    fwait(BANDS - 1)
    whiten(BANDS - 1)

    y2, yp, ym = (y + 2) % NY, (y + 1) % NY, (y + NY - 1) % NY
    turn = [y2, yp, ym, y]

    def piece(b):
        return pl.ds(b * PIECE, PIECE)

    def swap(b, i):
        k = turn[i]
        return remote(
            part.at[piece(b), k * 2 + 1 - c], other.at[k, piece(b)],
            csend.at[b, i], crecv.at[b, i], core,
        )

    def add_swap(b, i):
        swap(b, i).wait_recv()
        k = turn[i]

        def one(p, carry):
            mine[k, p] = (part[p, k * 2 + c].astype(F32) + other[k, p].astype(F32)).astype(BF16)
            return carry

        lax.fori_loop(b * PIECE, (b + 1) * PIECE, one, 0)

    nxt, bck = [yp, ym], [ym, yp]
    ahead, behind = [up, down], [down, up]

    def far(b):
        return remote(mine.at[y2, piece(b)], h.at[b], ysend.at[b, 0], yrecv.at[b, 0], ahead[b])

    def raw(b):
        return remote(
            mine.at[bck[b], piece(b)], v.at[b], ysend.at[b, 1], yrecv.at[b, 1], behind[b]
        )

    def near(b):
        return remote(
            mine.at[nxt[b], piece(b)], u.at[b], ysend.at[b, 2], yrecv.at[b, 2], ahead[b]
        )

    def to_far(b):
        add_swap(b, 0)
        far(b).start()
        back = 2 if b == 0 else 1
        add_swap(b, back)
        raw(b).start()
        add_swap(b, 3 - back)
        add_swap(b, 3)

    def to_near(b):
        far(b).wait_recv()
        k = nxt[b]

        def one(p, carry):
            mine[k, b * PIECE + p] = (
                mine[k, b * PIECE + p].astype(F32) + h[b, p].astype(F32)
            ).astype(BF16)
            return carry

        lax.fori_loop(0, PIECE, one, 0)
        near(b).start()

    def to_sums(b):
        raw(b).wait_recv()
        near(b).wait_recv()

        def one(p, carry):
            for g in range(2):
                i = g * SUBN + p
                t = mine[y, b * PIECE + i].astype(F32) + u[b, i].astype(F32) + v[b, i].astype(F32)
                for l in range(8):
                    sums[b, g * 8 + l, p] = t[:, l * TILE : (l + 1) * TILE]
            return carry

        lax.fori_loop(0, SUBN, one, 0)

    ups, downs = NZ // 2, NZ // 2 - 1

    def chain_up(s, b):
        src = sums.at[b, (z + ups) % NZ] if s == 0 else cp.at[b, s - 1]
        return remote(src, cp.at[b, s], psend.at[s, b], precv.at[s, b], zup)

    def chain_down(s, b):
        src = sums.at[b, (z + NZ - downs) % NZ] if s == 0 else cm.at[b, s - 1]
        return remote(src, cm.at[b, s], msend.at[s, b], mrecv.at[s, b], zdown)

    def link(s, b):
        if s:
            chain_up(s - 1, b).wait_recv()
            cp[b, s - 1] = cp[b, s - 1] + sums[b, (z + ups - s) % NZ]
        chain_up(s, b).start()
        if s and s < downs:
            chain_down(s - 1, b).wait_recv()
            cm[b, s - 1] = cm[b, s - 1] + sums[b, (z + NZ - downs + s) % NZ]
        if s < downs:
            chain_down(s, b).start()

    some_pairs(BANDS - 1, 0, PIECE)
    for i in range(NY):
        swap(0, i).start()
    some_pairs(BANDS - 1, PIECE, PIECE)
    for i in (0, 2, 1, 3):
        swap(1, i).start()
    to_far(0)
    to_far(1)
    to_near(0)
    to_near(1)
    to_sums(0)
    link(0, 0)
    to_sums(1)
    link(0, 1)
    for s in range(1, ups):
        for b in range(PIECES):
            link(s, b)
    for b in range(PIECES):
        chain_down(downs - 1, b).wait_recv()
        chain_up(ups - 1, b).wait_recv()
        final[b * SUBN : (b + 1) * SUBN] = (sums[b, z] + cp[b, ups - 1] + cm[b, downs - 1]).astype(
            BF16
        )
    final[HALF] = jnp.zeros((ROWS, TILE), BF16)

    def fill(o, carry):
        give[o] = final[sends[o]]
        return carry

    lax.fori_loop(0, owners, fill, 0)

    def deliver(d, carry):
        o = (chan + d) % owners
        remote(give.at[o], got.at[chan], gsend, grecv, {"chan": o}).start()
        return carry

    lax.fori_loop(1, owners, deliver, 0)
    got[chan] = give[chan]
    many = pl.ds(0, owners - 1)
    pltpu.make_async_copy(got.at[many], got.at[many], grecv).wait()

    for k in range(SLOTS):
        base, on = takes[0, k], takes[1, k]
        for l in range(8):
            t = got[base + l * NX].astype(F32)
            out[k, :, l * TILE : (l + 1) * TILE] = jnp.where(on > 0, t, 0.0)

    pltpu.make_async_copy(give.at[many], give.at[many], gsend).wait()
    for q in range(BANDS):
        sent = held.at[q, x, pl.ds(0, NZ - 1)]
        if RELAY:
            to_relay(q).wait_send()
            from_relay(q).wait_send()
            gone = held.at[q, x, pl.ds(0, NZ - 2)]
            pltpu.make_async_copy(gone, gone, zsend.at[q]).wait()
            gone = held.at[q, x, 0, low]
            pltpu.make_async_copy(gone, gone, zlow.at[q]).wait()
        else:
            pltpu.make_async_copy(sent, sent, zsend.at[q]).wait()
        for side in range(2):
            sent = held.at[q, x]
            pltpu.make_async_copy(sent, sent, xsend.at[q, side]).wait()
            sent = held.at[q, x, pl.ds(0, NZ // 2)]
            pltpu.make_async_copy(sent, sent, fsend.at[q, side]).wait()
    for b in range(PIECES):
        for i in range(NY):
            swap(b, i).wait_send()
        far(b).wait_send()
        raw(b).wait_send()
        near(b).wait_send()
        for s in range(ups):
            chain_up(s, b).wait_send()
        for s in range(downs):
            chain_down(s, b).wait_send()


def call_kernel(spectra, table, counts, cosine, sine, sends, takes):
    smem = pl.BlockSpec(memory_space=pltpu.SMEM)
    vmem = pl.BlockSpec(memory_space=pltpu.VMEM)
    dma = pltpu.SemaphoreType.DMA
    side = (ROWS, LAGS * BLK)
    tile = (SUBN, ROWS, TILE)
    ups = NZ // 2
    return pl.pallas_call(
        kernel,
        out_shape=jax.ShapeDtypeStruct((SLOTS, ROWS, LAGS * BLK), F32),
        in_specs=[vmem, smem, smem, vmem, vmem, smem, smem],
        out_specs=vmem,
        scratch_shapes=[
            pltpu.VMEM((BANDS, NX, NZ, BLK, WIDE), BF16),
            pltpu.VMEM((BANDS, BLK // 2, WIDE), BF16),
            pltpu.VMEM((NBLK, BLK, WIDE), BF16),
            pltpu.VMEM((2, LAGS * BLK, WIDE), BF16),
            pltpu.VMEM((MINE, BLK, LAGS * BLK), F32),
            pltpu.VMEM((MINE, BLK // ROWS, *side), BF16),
            pltpu.VMEM((NY, MINE, *side), BF16),
            pltpu.VMEM((NY, MINE, *side), BF16),
            pltpu.VMEM((PIECES, PIECE, *side), BF16),
            pltpu.VMEM((PIECES, PIECE, *side), BF16),
            pltpu.VMEM((PIECES, PIECE, *side), BF16),
            pltpu.VMEM((PIECES, NZ, *tile), F32),
            pltpu.VMEM((PIECES, ups, *tile), F32),
            pltpu.VMEM((PIECES, ups - 1, *tile), F32),
            pltpu.VMEM((HALF + 1, ROWS, TILE), BF16),
            pltpu.VMEM((NBLK, ROWS, TILE), BF16),
            pltpu.VMEM((NBLK, ROWS, TILE), BF16),
            dma((BANDS,)),
            dma((BANDS,)), dma((BANDS,)), dma((BANDS, 4)),
            dma((BANDS,)), dma((BANDS,)), dma((BANDS,)),
            dma((BANDS, 2)), dma((BANDS, 4, 2)),
            dma((BANDS, 2)), dma((BANDS, 2)),
            dma((PIECES, NY)), dma((PIECES, NY)),
            dma((PIECES, 3)), dma((PIECES, 3)),
            dma((ups, PIECES)), dma((ups, PIECES)),
            dma((ups - 1, PIECES)), dma((ups - 1, PIECES)),
            dma, dma,
        ],
        compiler_params=pltpu.CompilerParams(
            collective_id=0, has_side_effects=True, vmem_limit_bytes=58 << 20
        ),
        name="stack",
    )(spectra, table, counts, cosine, sine, sends, takes)


def phase_tables(z):
    band = z * BANDS + jnp.arange(BANDS, dtype=jnp.int32)
    freq = band[:, None, None] * BAND + jnp.arange(BAND, dtype=jnp.int32)[None, None, :]
    lag = jnp.arange(LAGS, dtype=jnp.int32)[None, :, None] - LAGS // 2
    phase = jnp.mod(lag * freq, 2 * F)
    angle = jnp.pi * phase.astype(F32) / F
    c, s = jnp.cos(angle), jnp.sin(angle)
    return jnp.concatenate([c, c], -1), jnp.concatenate([s, -s], -1)


def plans(pairs, chan):
    z, x = chan // NX, chan % NX
    owners = pairs[:, 2]
    places = jnp.arange(NPAIRS, dtype=jnp.int32)
    before = (owners[None, :] < owners[:, None]) | (
        (owners[None, :] == owners[:, None]) & (places[None, :] < places[:, None])
    )
    rank = jnp.sum(before.astype(jnp.int32), axis=1)
    i = places[:MINE]
    spot = i // (2 * SUBN) * SUBN + i % SUBN
    wanted = spot * 8 + i // SUBN % 2 * 4 + x
    pick = (rank[None, :] == wanted[:, None]).astype(jnp.int32)
    table = jnp.sum(pick[None] * pairs.T[:2, None, :], axis=2)

    ids = jnp.arange(NBLK, dtype=jnp.int32)
    first = jnp.sum((owners[None, :] < ids[:, None]).astype(jnp.int32), axis=1)
    count = jnp.sum((owners[None, :] == ids[:, None]).astype(jnp.int32), axis=1)
    bin_ = z // 8 * 4 + x
    ahead = jnp.mod(bin_ - first, 8)
    sends = jnp.where(ahead < count, (first + ahead) // 8, HALF)

    me = (ids == chan).astype(jnp.int32)
    r = jnp.sum(me * first) + jnp.arange(SLOTS, dtype=jnp.int32)
    on = (jnp.arange(SLOTS, dtype=jnp.int32) < jnp.sum(me * count)).astype(jnp.int32)
    base = r % 8 // 4 * (8 * NX) + r % 4
    return table, sends, jnp.stack([base, on])


def per_device(spectra, block_counts, pairs):
    chan = lax.axis_index("chan")
    cosine, sine = phase_tables(chan // NX)
    table, sends, takes = plans(pairs, chan)
    return call_kernel(spectra, table, block_counts, cosine, sine, sends, takes)


def solution(mesh):
    placed = (P("tm", "chan", None), P(), P())
    return jax.shard_map(
        per_device, mesh=mesh, in_specs=placed, out_specs=P("chan", "tm", None), check_vma=False
    )
```

```python
import jax
import jax.numpy as jnp
import numpy as np
from jax import lax
from jax.experimental import pallas as pl
from jax.experimental.pallas import tpu as pltpu
from jax.sharding import PartitionSpec as P

F = 4096
BAND = 64
BLK = 128
LAGS = 8
SLOTS = 3
NBLK = 64
NPAIRS = 96
SCALE = 1.0 / 256.0
MESH = pl.DeviceIdType.MESH
BF16 = jnp.bfloat16
F32 = jnp.float32

NZ, NX, NY = 16, 4, 4
BANDS = F // BAND // NZ
WIDE = 2 * BAND
MINE = NPAIRS // NX
PIECES = (4, 4, 4, 4, 3, 3, 1, 1)
FIRST = tuple(sum(PIECES[:b]) for b in range(len(PIECES)))
QUAD = 4
ROWS = 16
TROW, TCOL = 8, 128
TALL, FLAT = ROWS // TROW, LAGS * BLK // TCOL

GROUPS = ((0, 1, 15, 2), (14, 3, 13, 4), (12, 5, 11, 6), (10, 7, 9, 8))
LAST = GROUPS[:3] + ((10, 7), (9, 8))


def groups_of(q):
    return LAST if q == BANDS - 1 else GROUPS


def place():
    tm, chan = lax.axis_index("tm"), lax.axis_index("chan")
    return tm // 2, tm % 2, chan // NX, chan % NX


def remote(src, dst, send, recv, where):
    return pltpu.make_async_remote_copy(
        src_ref=src, dst_ref=dst, send_sem=send, recv_sem=recv, device_id=where, device_id_type=MESH
    )


def bytes_of(ref, sem):
    pltpu.make_async_copy(ref, ref, sem).wait()


def kernel(
    spectra, phases, table, ranks, counts, out,
    spec, trig, held0, held1, held2, held3, moved, acc, part, mine, other, h, u, v,
    sums, sent1, got1, sum2, sent2, got2, final, give, got,
    local, zsend, zrecv, xsend, xrecv, fsend, frecv,
    csend, crecv, ysend, yrecv, send1, recv1, send2, recv2, gsend, grecv,
):
    y, c, z, x = place()
    chan = lax.axis_index("chan")
    owners = NZ * NX
    xl, xr = (x + NX - 1) % NX, (x + 1) % NX
    right, left = {"chan": z * NX + xr}, {"chan": z * NX + xl}
    core = {"tm": y * 2 + 1 - c}
    up, down = {"tm": (y + 1) % NY * 2 + c}, {"tm": (y + NY - 1) % NY * 2 + c}
    opposite = {"chan": z * NX + (x + 2) % NX}
    held = (held0, held1, held2, held3)

    def slot(xs, zs):
        return xs * NZ + zs

    def slots(xs, n):
        return pl.ds(xs * NZ, n)

    load = pltpu.make_async_copy(spectra.at[0], spec, local.at[BANDS])
    load.start()
    load_trig = pltpu.make_async_copy(phases.at[z], trig, local.at[BANDS + 1])
    load_trig.start()

    barrier = pltpu.get_barrier_semaphore()
    for where in (core, up, down):
        pl.semaphore_signal(barrier, inc=1, device_id=where, device_id_type=MESH)

    def greet(d, carry):
        pl.semaphore_signal(
            barrier, inc=1, device_id={"chan": (chan + d) % owners}, device_id_type=MESH
        )
        return carry

    lax.fori_loop(1, owners, greet, 0)
    load.wait()
    load_trig.wait()
    alive = (lax.broadcasted_iota(jnp.int32, (BLK, WIDE), 0) < counts[chan]).astype(F32)

    def whiten(i, carry):
        cols = pl.ds(pl.multiple_of(i * WIDE, WIDE), WIDE)
        t = spec[:, cols].astype(F32)
        power = jnp.sum(t * t, axis=-1, keepdims=True) * (1.0 / BAND)
        spec[:, cols] = (t * lax.rsqrt(power + 1e-06) * alive).astype(BF16)
        return carry

    lax.fori_loop(0, F // BAND, whiten, 0)
    pl.semaphore_wait(barrier, owners + 2)

    def columns(zt, q):
        return spec.at[:, pl.ds(pl.multiple_of((zt * BANDS + q) * WIDE, WIDE), WIDE)]

    def own(q):
        return pltpu.make_async_copy(columns(z, q), held[q].at[slot(x, z)], local.at[q])

    def zsends(q):
        for j, group in enumerate(groups_of(q)):
            for d in group:
                if d:
                    zt = (z + d) % NZ
                    remote(
                        columns(zt, q), held[q].at[slot(x, z)], zsend.at[q], zrecv.at[q, j],
                        {"chan": zt * NX + x},
                    ).start()

    def zwait(q, j):
        n = len(groups_of(q)[j])
        if j == 0:
            own(q).wait()
            n -= 1
        bytes_of(held[q].at[slots(x, n)], zrecv.at[q, j])

    def direct(q, j):
        return q == BANDS - 1 and j >= 3

    def xstart(q, j):
        for d in groups_of(q)[j]:
            blk = held[q].at[slot(x, (z + NZ - d) % NZ)]
            remote(blk, blk, xsend.at[q, 0], xrecv.at[q, j, 0], right).start()
            remote(blk, blk, xsend.at[q, 1], xrecv.at[q, j, 1], left).start()
            if direct(q, j):
                remote(blk, blk, fsend.at[q, 2], frecv.at[q, 2], opposite).start()

    def forward(q, j):
        group = groups_of(q)[j]
        n = len(group)
        for side, (xs, where) in enumerate(((xl, right), (xr, left))):
            bytes_of(held[q].at[slots(xs, n)], xrecv.at[q, j, side])
            if not direct(q, j):
                for d in group[side * n // 2 : (side + 1) * n // 2]:
                    blk = held[q].at[slot(xs, (z + NZ - d) % NZ)]
                    remote(blk, blk, fsend.at[q, side], frecv.at[q, side], where).start()

    def passed(q):
        return 6 if q == BANDS - 1 else 8

    def fwait(q):
        for side in range(2):
            bytes_of(held[q].at[slots(x, passed(q))], frecv.at[q, side])
        if q == BANDS - 1:
            bytes_of(held[q].at[slots(x, 4)], frecv.at[q, 2])

    def pair(q, p, slot):
        t = held[q][table[1, p]].astype(F32)
        w = pltpu.roll(t, BAND, 1)
        for m in range(LAGS):
            moved[slot, m * BLK : (m + 1) * BLK] = (
                t * trig[0, q, m : m + 1, :] + w * trig[1, q, m : m + 1, :]
            ).astype(BF16)
        corr = lax.dot_general(
            held[q][table[0, p]], moved[slot], (((1,), (1,)), ((), ())),
            preferred_element_type=F32,
        )
        if q == 0:
            acc[p] = corr
        elif q < BANDS - 1:
            acc[p] = acc[p] + corr
        else:
            acc[p] = (acc[p] + corr) * SCALE
            for k in range(NY):
                part[p, k] = acc[p, rows(k, 1 - c)].astype(BF16)

    def rows(k, core_):
        return pl.ds(pl.multiple_of((k * 2 + core_) * ROWS, ROWS), ROWS)

    def some_pairs(q, first, count):
        def one(i, carry):
            for slot in range(2):
                pair(q, first + i * 2 + slot, slot)
            return carry

        lax.fori_loop(0, count // 2, one, 0)

    for q in range(BANDS):
        own(q).start()
        zsends(q)

    third = MINE // 3
    prev = None
    for q in range(BANDS):
        for j in range(len(groups_of(q))):
            zwait(q, j)
            xstart(q, j)
            if prev is not None:
                forward(*prev)
            prev = (q, j)
            if q and j == 1:
                fwait(q - 1)
                some_pairs(q - 1, 0, third)
            elif q and j == 2:
                some_pairs(q - 1, third, 2 * third)
    end = BANDS - 1
    forward(*prev)
    fwait(end)

    y2, yp, ym = (y + 2) % NY, (y + 1) % NY, (y + NY - 1) % NY
    turn = [y2, yp, ym, y]

    def piece(b):
        return pl.ds(FIRST[b], PIECES[b])

    def swap(b, i):
        k = turn[i]
        return remote(
            part.at[piece(b), k], other.at[k, piece(b)], csend.at[b, i], crecv.at[b, i], core
        )

    def swaps(b):
        for i in range(NY):
            swap(b, i).start()

    def add_swap(b, i):
        swap(b, i).wait_recv()
        k = turn[i]

        def one(p, carry):
            mine[k, p] = (acc[p, rows(k, c)] + other[k, p].astype(F32)).astype(BF16)
            return carry

        lax.fori_loop(FIRST[b], FIRST[b] + PIECES[b], one, 0)

    nxt, bck = [yp, ym], [ym, yp]
    ahead, behind = [up, down], [down, up]

    def far(b):
        return remote(mine.at[y2, piece(b)], h.at[piece(b)], ysend.at[b, 0], yrecv.at[b, 0], ahead[b % 2])

    def raw(b):
        return remote(
            mine.at[bck[b % 2], piece(b)], v.at[piece(b)], ysend.at[b, 1], yrecv.at[b, 1], behind[b % 2]
        )

    def near(b):
        return remote(
            mine.at[nxt[b % 2], piece(b)], u.at[piece(b)], ysend.at[b, 2], yrecv.at[b, 2], ahead[b % 2]
        )

    def to_far(b):
        add_swap(b, 0)
        far(b).start()
        back = 2 - b % 2
        add_swap(b, back)
        raw(b).start()
        add_swap(b, 3 - back)
        add_swap(b, 3)

    def to_near(b):
        far(b).wait_recv()
        k = nxt[b % 2]

        def one(p, carry):
            mine[k, p] = (mine[k, p].astype(F32) + h[p].astype(F32)).astype(BF16)
            return carry

        lax.fori_loop(FIRST[b], FIRST[b] + PIECES[b], one, 0)
        near(b).start()

    four, at = z // QUAD, z % QUAD

    def near_z(b, k):
        m = (at + k) % QUAD
        return remote(
            sent1.at[m, :, piece(b)], got1.at[k - 1, :, piece(b)], send1.at[b, k - 1],
            recv1.at[b, k - 1], {"chan": (four * QUAD + m) * NX + x},
        )

    def far_z(b, k):
        f = (four + k) % QUAD
        return remote(
            sent2.at[f, piece(b)], got2.at[k - 1, piece(b)], send2.at[b, k - 1],
            recv2.at[b, k - 1], {"chan": (f * QUAD + at) * NX + x},
        )

    def to_sums(b):
        raw(b).wait_recv()
        near(b).wait_recv()

        def one(p, carry):
            t = mine[y, p].astype(F32) + u[p].astype(F32) + v[p].astype(F32)
            for i in range(NZ):
                r, l = i // FLAT, i % FLAT
                tile = t[r * TROW : (r + 1) * TROW, l * TCOL : (l + 1) * TCOL]
                sums[i % QUAD, i // QUAD, p] = tile
                sent1[i % QUAD, i // QUAD, p] = tile.astype(BF16)
            return carry

        lax.fori_loop(FIRST[b], FIRST[b] + PIECES[b], one, 0)
        for k in range(1, QUAD):
            near_z(b, k).start()

    def to_far_z(b):
        for k in range(1, QUAD):
            near_z(b, k).wait_recv()
        for f in range(QUAD):
            t = sums[at, f, piece(b)]
            for k in range(QUAD - 1):
                t = t + got1[k, f, piece(b)].astype(F32)
            sum2[f, piece(b)] = t
            sent2[f, piece(b)] = t.astype(BF16)
        for k in range(1, QUAD):
            far_z(b, k).start()

    def to_final(b):
        t = sum2[four, piece(b)]
        for k in range(1, QUAD):
            far_z(b, k).wait_recv()
            t = t + got2[k - 1, piece(b)].astype(F32)
        final[piece(b)] = t.astype(final.dtype)

    def both(stage, *couples):
        for g in couples:
            stage(2 * g)
            stage(2 * g + 1)

    def compute(b):
        some_pairs(end, FIRST[b], PIECES[b] + PIECES[b + 1])
        swaps(b)
        swaps(b + 1)

    compute(0)
    compute(2)
    both(to_far, 0)
    compute(4)
    compute(6)
    both(to_near, 0)
    both(to_far, 1)
    both(to_sums, 0)
    both(to_near, 1)
    both(to_far, 2)
    both(to_far_z, 0)
    both(to_sums, 1)
    both(to_near, 2)
    both(to_far, 3)
    both(to_far_z, 1)
    both(to_sums, 2)
    both(to_near, 3)
    both(to_far_z, 2)
    both(to_sums, 3)
    both(to_far_z, 3)
    both(to_final, 0, 1, 2, 3)
    final[MINE] = jnp.zeros((TROW, TCOL), final.dtype)

    def fill(o):
        first = ranks[NPAIRS + o]
        count = ranks[NPAIRS + o + 1] - first
        skip = (x + 4 * NPAIRS - first) % NX
        give[o] = final[jnp.where(skip < count, (first + skip) // NX, MINE)]

    def deliver(d, carry):
        o = (chan + d) % owners
        fill(o)
        remote(give.at[o], got.at[chan], gsend, grecv, {"chan": o}).start()
        return carry

    lax.fori_loop(1, owners, deliver, 0)
    fill(chan)
    got[chan] = give[chan]
    many = pl.ds(0, owners - 1)
    bytes_of(got.at[many], grecv)

    first = ranks[NPAIRS + chan]
    count = ranks[NPAIRS + chan + 1] - first
    for k in range(SLOTS):
        group = (first + k) % NX
        for r in range(TALL):
            for l in range(FLAT):
                t = got[(r * FLAT + l) * NX + group].astype(F32)
                out[k, r * TROW : (r + 1) * TROW, l * TCOL : (l + 1) * TCOL] = jnp.where(
                    k < count, t, 0.0
                )

    bytes_of(give.at[many], gsend)
    for q in range(BANDS):
        bytes_of(held[q].at[slots(x, NZ - 1)], zsend.at[q])
        for side in range(2):
            bytes_of(held[q].at[slots(x, NZ)], xsend.at[q, side])
            bytes_of(held[q].at[slots(x, passed(q))], fsend.at[q, side])
        if q == BANDS - 1:
            bytes_of(held[q].at[slots(x, 4)], fsend.at[q, 2])
    for b in range(len(PIECES)):
        for i in range(NY):
            swap(b, i).wait_send()
        far(b).wait_send()
        raw(b).wait_send()
        near(b).wait_send()
        for k in range(1, QUAD):
            near_z(b, k).wait_send()
            far_z(b, k).wait_send()


def call_kernel(spectra, phases, table, ranks, counts):
    smem = pl.BlockSpec(memory_space=pltpu.SMEM)
    vmem = pl.BlockSpec(memory_space=pltpu.VMEM)
    hbm = pl.BlockSpec(memory_space=pl.ANY)
    dma = pltpu.SemaphoreType.DMA
    side = (ROWS, LAGS * BLK)
    tiles = (QUAD, MINE, TROW, TCOL)
    block = pltpu.VMEM((NBLK, BLK, WIDE), BF16)
    n = len(PIECES)
    return pl.pallas_call(
        kernel,
        out_shape=jax.ShapeDtypeStruct((SLOTS, ROWS, LAGS * BLK), F32),
        in_specs=[hbm, hbm, smem, smem, smem],
        out_specs=vmem,
        scratch_shapes=[
            pltpu.VMEM((BLK, 2 * F), BF16),
            pltpu.VMEM((2, BANDS, LAGS, WIDE), F32),
            block, block, block, block,
            pltpu.VMEM((2, LAGS * BLK, WIDE), BF16),
            pltpu.VMEM((MINE, BLK, LAGS * BLK), F32),
            pltpu.VMEM((MINE, NY, *side), BF16),
            pltpu.VMEM((NY, MINE, *side), BF16),
            pltpu.VMEM((NY, MINE, *side), BF16),
            pltpu.VMEM((MINE, *side), BF16),
            pltpu.VMEM((MINE, *side), BF16),
            pltpu.VMEM((MINE, *side), BF16),
            pltpu.VMEM((QUAD, *tiles), F32),
            pltpu.VMEM((QUAD, *tiles), BF16),
            pltpu.VMEM((QUAD - 1, *tiles), BF16),
            pltpu.VMEM(tiles, F32),
            pltpu.VMEM(tiles, BF16),
            pltpu.VMEM((QUAD - 1, *tiles[1:]), BF16),
            pltpu.VMEM((MINE + 1, TROW, TCOL), BF16),
            pltpu.VMEM((NBLK, TROW, TCOL), BF16),
            pltpu.VMEM((NBLK, TROW, TCOL), BF16),
            dma((BANDS + 2,)),
            dma((BANDS,)), dma((BANDS, 5)),
            dma((BANDS, 2)), dma((BANDS, 5, 2)),
            dma((BANDS, 3)), dma((BANDS, 3)),
            dma((n, NY)), dma((n, NY)),
            dma((n, 3)), dma((n, 3)),
            dma((n, QUAD - 1)), dma((n, QUAD - 1)),
            dma((n, QUAD - 1)), dma((n, QUAD - 1)),
            dma, dma,
        ],
        compiler_params=pltpu.CompilerParams(
            collective_id=0, has_side_effects=True, vmem_limit_bytes=58 << 20
        ),
        name="stack",
    )(spectra, phases, table, ranks, counts)


def phase_tables():
    freq = np.arange(F, dtype=np.int32).reshape(NZ, BANDS, 1, BAND)
    lag = np.arange(LAGS, dtype=np.int32)[:, None] - LAGS // 2
    phase = np.mod(lag * freq, 2 * F)
    angle = np.float32(np.pi) * phase.astype(np.float32) / np.float32(F)
    c, s = np.cos(angle), np.sin(angle)
    return np.stack([np.concatenate([c, c], -1), np.concatenate([s, -s], -1)], axis=1)


def plans(pairs, x):
    places = jnp.arange(NPAIRS, dtype=jnp.int32)
    keys = pairs[:, 2] * NPAIRS + places
    asked = jnp.concatenate([keys, jnp.arange(NBLK + 1, dtype=jnp.int32) * NPAIRS])
    ranks = jnp.sum((keys[None, :] < asked[:, None]).astype(jnp.int32), axis=1)
    wanted = places[:MINE] * NX + x
    pick = (ranks[None, :NPAIRS] == wanted[:, None]).astype(jnp.int32)
    blocks = pairs.T[:2]
    blocks = blocks % NX * NZ + blocks // NX
    return jnp.sum(pick[None] * blocks[:, None, :], axis=2), ranks


def per_device(spectra, block_counts, pairs):
    table, ranks = plans(pairs, lax.axis_index("chan") % NX)
    return call_kernel(spectra, jnp.asarray(phase_tables()), table, ranks, block_counts)


def solution(mesh):
    placed = (P("tm", "chan", None), P(), P())
    return jax.shard_map(
        per_device, mesh=mesh, in_specs=placed, out_specs=P("chan", "tm", None), check_vma=False
    )
```

```python
import jax
import jax.numpy as jnp
import numpy as np
from jax import lax
from jax.experimental import pallas as pl
from jax.experimental.pallas import tpu as pltpu
from jax.sharding import PartitionSpec as P

F = 4096
BAND = 64
BLK = 128
LAGS = 8
SLOTS = 3
NBLK = 64
NPAIRS = 96
SCALE = 1.0 / 256.0
MESH = pl.DeviceIdType.MESH
BF16 = jnp.bfloat16
F32 = jnp.float32

NZ, NX, NY = 16, 4, 4
BANDS = F // BAND // NZ
WIDE = 2 * BAND
MINE = NPAIRS // NX
PIECES = (2, 2, 3, 3, 3, 3, 4, 4)
FIRST = tuple(sum(PIECES[:b]) for b in range(len(PIECES)))
QUAD = 4
ROWS = 16
TROW, TCOL = 8, 128
TALL, FLAT = ROWS // TROW, LAGS * BLK // TCOL

GROUPS = ((0, 1, 15, 2), (14, 3, 13, 4), (12, 5, 11, 6), (10, 7, 9, 8))
LAST = GROUPS[:3] + ((10, 7), (9, 8))


def groups_of(q):
    return LAST if q == BANDS - 1 else GROUPS


def place():
    tm, chan = lax.axis_index("tm"), lax.axis_index("chan")
    return tm // 2, tm % 2, chan // NX, chan % NX


def remote(src, dst, send, recv, where):
    return pltpu.make_async_remote_copy(
        src_ref=src, dst_ref=dst, send_sem=send, recv_sem=recv, device_id=where, device_id_type=MESH
    )


def bytes_of(ref, sem):
    pltpu.make_async_copy(ref, ref, sem).wait()


def kernel(
    spectra, phases, table, ranks, counts, out,
    spec, trig, held0, held1, held2, held3, moved, acc, part, mine, other, h, u, v,
    sums, sent1, got1, sum2, sent2, got2, final, give, got, spot,
    local, zsend, zrecv, xsend, xrecv, fsend, frecv,
    csend, crecv, ysend, yrecv, send1, recv1, send2, recv2, gsend, grecv,
):
    y, c, z, x = place()
    chan = lax.axis_index("chan")
    owners = NZ * NX
    xl, xr = (x + NX - 1) % NX, (x + 1) % NX
    right, left = {"chan": z * NX + xr}, {"chan": z * NX + xl}
    core = {"tm": y * 2 + 1 - c}
    up, down = {"tm": (y + 1) % NY * 2 + c}, {"tm": (y + NY - 1) % NY * 2 + c}
    opposite = {"chan": z * NX + (x + 2) % NX}
    held = (held0, held1, held2, held3)

    def slot(xs, zs):
        return xs * NZ + zs

    def slots(xs, n):
        return pl.ds(xs * NZ, n)

    load = pltpu.make_async_copy(spectra.at[0], spec, local.at[BANDS])
    load.start()
    load_trig = pltpu.make_async_copy(phases.at[z], trig, local.at[BANDS + 1])
    load_trig.start()

    barrier = pltpu.get_barrier_semaphore()
    for where in (core, up, down):
        pl.semaphore_signal(barrier, inc=1, device_id=where, device_id_type=MESH)

    def greet(d, carry):
        pl.semaphore_signal(
            barrier, inc=1, device_id={"chan": (chan + d) % owners}, device_id_type=MESH
        )
        return carry

    lax.fori_loop(1, owners, greet, 0)
    load.wait()
    load_trig.wait()
    alive = (lax.broadcasted_iota(jnp.int32, (BLK, WIDE), 0) < counts[chan]).astype(F32)

    def whiten(q):
        def one(zt, carry):
            cols = pl.ds(pl.multiple_of((zt * BANDS + q) * WIDE, WIDE), WIDE)
            t = spec[:, cols].astype(F32)
            power = jnp.sum(t * t, axis=-1, keepdims=True) * (1.0 / BAND)
            spec[:, cols] = (t * lax.rsqrt(power + 1e-06) * alive).astype(BF16)
            return carry

        lax.fori_loop(0, NZ, one, 0)

    whiten(0)
    pl.semaphore_wait(barrier, owners + 2)

    def columns(zt, q):
        return spec.at[:, pl.ds(pl.multiple_of((zt * BANDS + q) * WIDE, WIDE), WIDE)]

    def own(q):
        return pltpu.make_async_copy(columns(z, q), held[q].at[slot(x, z)], local.at[q])

    def zsends(q):
        for j, group in enumerate(groups_of(q)):
            for d in group:
                if d:
                    zt = (z + d) % NZ
                    remote(
                        columns(zt, q), held[q].at[slot(x, z)], zsend.at[q], zrecv.at[q, j],
                        {"chan": zt * NX + x},
                    ).start()

    def zwait(q, j):
        n = len(groups_of(q)[j])
        if j == 0:
            own(q).wait()
            n -= 1
        bytes_of(held[q].at[slots(x, n)], zrecv.at[q, j])

    def direct(q, j):
        return q == BANDS - 1 and j >= 3

    def xstart(q, j):
        for d in groups_of(q)[j]:
            blk = held[q].at[slot(x, (z + NZ - d) % NZ)]
            remote(blk, blk, xsend.at[q, 0], xrecv.at[q, j, 0], right).start()
            remote(blk, blk, xsend.at[q, 1], xrecv.at[q, j, 1], left).start()
            if direct(q, j):
                remote(blk, blk, fsend.at[q, 2], frecv.at[q, 2], opposite).start()

    def forward(q, j):
        group = groups_of(q)[j]
        n = len(group)
        for side, (xs, where) in enumerate(((xl, right), (xr, left))):
            bytes_of(held[q].at[slots(xs, n)], xrecv.at[q, j, side])
            if not direct(q, j):
                for d in group[side * n // 2 : (side + 1) * n // 2]:
                    blk = held[q].at[slot(xs, (z + NZ - d) % NZ)]
                    remote(blk, blk, fsend.at[q, side], frecv.at[q, side], where).start()

    def passed(q):
        return 6 if q == BANDS - 1 else 8

    def fwait(q):
        for side in range(2):
            bytes_of(held[q].at[slots(x, passed(q))], frecv.at[q, side])
        if q == BANDS - 1:
            bytes_of(held[q].at[slots(x, 4)], frecv.at[q, 2])

    def pair(q, p, slot):
        t = held[q][table[1, p]].astype(F32)
        w = pltpu.roll(t, BAND, 1)
        for m in range(LAGS):
            moved[slot, m * BLK : (m + 1) * BLK] = (
                t * trig[0, q, m : m + 1, :] + w * trig[1, q, m : m + 1, :]
            ).astype(BF16)
        corr = lax.dot_general(
            held[q][table[0, p]], moved[slot], (((1,), (1,)), ((), ())),
            preferred_element_type=F32,
        )
        if q == 0:
            acc[p] = corr
        elif q < BANDS - 1:
            acc[p] = acc[p] + corr
        else:
            acc[p] = (acc[p] + corr) * SCALE
            for k in range(NY):
                part[p, k] = acc[p, rows(k, 1 - c)].astype(BF16)

    def rows(k, core_):
        return pl.ds(pl.multiple_of((k * 2 + core_) * ROWS, ROWS), ROWS)

    def some_pairs(q, first, count):
        def one(i, carry):
            for slot in range(2):
                pair(q, first + i * 2 + slot, slot)
            return carry

        lax.fori_loop(0, count // 2, one, 0)

    for q in range(BANDS):
        own(q).start()
        zsends(q)
        if q < BANDS - 1:
            whiten(q + 1)

    def find(o, carry):
        first = ranks[NPAIRS + o]
        count = ranks[NPAIRS + o + 1] - first
        skip = (x + 4 * NPAIRS - first) % NX
        spot[o] = jnp.where(skip < count, (first + skip) // NX, MINE)
        return carry

    lax.fori_loop(0, owners, find, 0)

    third = MINE // 3
    prev = None
    for q in range(BANDS):
        for j in range(len(groups_of(q))):
            zwait(q, j)
            xstart(q, j)
            if prev is not None:
                forward(*prev)
            prev = (q, j)
            if q and j == 1:
                fwait(q - 1)
                some_pairs(q - 1, 0, third)
            elif q and j == 2:
                some_pairs(q - 1, third, 2 * third)
    end = BANDS - 1
    forward(*prev)
    fwait(end)

    y2, yp, ym = (y + 2) % NY, (y + 1) % NY, (y + NY - 1) % NY
    turn = [y2, yp, ym, y]

    def piece(b):
        return pl.ds(FIRST[b], PIECES[b])

    def swap(b, i):
        k = turn[i]
        return remote(
            part.at[piece(b), k], other.at[k, piece(b)], csend.at[b, i], crecv.at[b, i], core
        )

    def swaps(b):
        for i in range(NY):
            swap(b, i).start()

    def add_swap(b, i):
        swap(b, i).wait_recv()
        k = turn[i]

        def one(p, carry):
            mine[k, p] = (acc[p, rows(k, c)] + other[k, p].astype(F32)).astype(BF16)
            return carry

        lax.fori_loop(FIRST[b], FIRST[b] + PIECES[b], one, 0)

    nxt, bck = [yp, ym], [ym, yp]
    ahead, behind = [up, down], [down, up]

    def far(b):
        return remote(mine.at[y2, piece(b)], h.at[piece(b)], ysend.at[b, 0], yrecv.at[b, 0], ahead[b % 2])

    def raw(b):
        return remote(
            mine.at[bck[b % 2], piece(b)], v.at[piece(b)], ysend.at[b, 1], yrecv.at[b, 1], behind[b % 2]
        )

    def near(b):
        return remote(
            mine.at[nxt[b % 2], piece(b)], u.at[piece(b)], ysend.at[b, 2], yrecv.at[b, 2], ahead[b % 2]
        )

    def to_far(b):
        add_swap(b, 0)
        far(b).start()
        back = 2 - b % 2
        add_swap(b, back)
        raw(b).start()
        add_swap(b, 3 - back)
        add_swap(b, 3)

    def to_near(b):
        far(b).wait_recv()
        k = nxt[b % 2]

        def one(p, carry):
            mine[k, p] = (mine[k, p].astype(F32) + h[p].astype(F32)).astype(BF16)
            return carry

        lax.fori_loop(FIRST[b], FIRST[b] + PIECES[b], one, 0)
        near(b).start()

    four, at = z // QUAD, z % QUAD

    def near_z(b, k):
        m = (at + k) % QUAD
        return remote(
            sent1.at[m, :, piece(b)], got1.at[k - 1, :, piece(b)], send1.at[b, k - 1],
            recv1.at[b, k - 1], {"chan": (four * QUAD + m) * NX + x},
        )

    def far_z(b, k):
        f = (four + k) % QUAD
        return remote(
            sent2.at[f, piece(b)], got2.at[k - 1, piece(b)], send2.at[b, k - 1],
            recv2.at[b, k - 1], {"chan": (f * QUAD + at) * NX + x},
        )

    def to_sums(b):
        raw(b).wait_recv()
        near(b).wait_recv()

        def one(p, carry):
            t = mine[y, p].astype(F32) + u[p].astype(F32) + v[p].astype(F32)
            for i in range(NZ):
                r, l = i // FLAT, i % FLAT
                tile = t[r * TROW : (r + 1) * TROW, l * TCOL : (l + 1) * TCOL]
                sums[i % QUAD, i // QUAD, p] = tile
                sent1[i % QUAD, i // QUAD, p] = tile.astype(BF16)
            return carry

        lax.fori_loop(FIRST[b], FIRST[b] + PIECES[b], one, 0)
        for k in range(1, QUAD):
            near_z(b, k).start()

    def to_far_z(b):
        for k in range(1, QUAD):
            near_z(b, k).wait_recv()
        for f in range(QUAD):
            t = sums[at, f, piece(b)]
            for k in range(QUAD - 1):
                t = t + got1[k, f, piece(b)].astype(F32)
            sum2[f, piece(b)] = t
            sent2[f, piece(b)] = t.astype(BF16)
        for k in range(1, QUAD):
            far_z(b, k).start()

    def to_final(b):
        t = sum2[four, piece(b)]
        for k in range(1, QUAD):
            far_z(b, k).wait_recv()
            t = t + got2[k - 1, piece(b)].astype(F32)
        final[piece(b)] = t.astype(final.dtype)

    def both(stage, *couples):
        for g in couples:
            stage(2 * g)
            stage(2 * g + 1)

    def compute(b):
        some_pairs(end, FIRST[b], PIECES[b] + PIECES[b + 1])
        swaps(b)
        swaps(b + 1)

    couples = len(PIECES) // 2
    compute(0)
    compute(2)
    both(to_far, 0)
    for g in range(2, couples):
        compute(2 * g)
    for g in range(couples):
        both(to_near, g)
        if g + 1 < couples:
            both(to_far, g + 1)
        if g:
            both(to_far_z, g - 1)
        both(to_sums, g)
    both(to_far_z, couples - 1)
    both(to_final, *range(couples))
    final[MINE] = jnp.zeros((TROW, TCOL), final.dtype)

    def fill(o):
        give[o] = final[spot[o]]

    def deliver(k, carry):
        zt = (z + 8 + (1 - 2 * (k % 2)) * ((k + 1) // 2)) % NZ
        for xt in range(NX):
            o = zt * NX + xt
            fill(o)
            remote(give.at[o], got.at[chan], gsend, grecv, {"chan": o}).start()
        return carry

    lax.fori_loop(0, NZ - 1, deliver, 0)
    for k in range(1, NX):
        o = z * NX + (x + k) % NX
        fill(o)
        remote(give.at[o], got.at[chan], gsend, grecv, {"chan": o}).start()
    fill(chan)
    got[chan] = give[chan]
    many = pl.ds(0, owners - 1)
    bytes_of(got.at[many], grecv)

    first = ranks[NPAIRS + chan]
    count = ranks[NPAIRS + chan + 1] - first
    for k in range(SLOTS):
        group = (first + k) % NX
        for r in range(TALL):
            for l in range(FLAT):
                t = got[(r * FLAT + l) * NX + group].astype(F32)
                out[k, r * TROW : (r + 1) * TROW, l * TCOL : (l + 1) * TCOL] = jnp.where(
                    k < count, t, 0.0
                )

    bytes_of(give.at[many], gsend)
    for q in range(BANDS):
        bytes_of(held[q].at[slots(x, NZ - 1)], zsend.at[q])
        for side in range(2):
            bytes_of(held[q].at[slots(x, NZ)], xsend.at[q, side])
            bytes_of(held[q].at[slots(x, passed(q))], fsend.at[q, side])
        if q == BANDS - 1:
            bytes_of(held[q].at[slots(x, 4)], fsend.at[q, 2])
    for b in range(len(PIECES)):
        for i in range(NY):
            swap(b, i).wait_send()
        far(b).wait_send()
        raw(b).wait_send()
        near(b).wait_send()
        for k in range(1, QUAD):
            near_z(b, k).wait_send()
            far_z(b, k).wait_send()


def call_kernel(spectra, phases, table, ranks, counts):
    smem = pl.BlockSpec(memory_space=pltpu.SMEM)
    vmem = pl.BlockSpec(memory_space=pltpu.VMEM)
    hbm = pl.BlockSpec(memory_space=pl.ANY)
    dma = pltpu.SemaphoreType.DMA
    side = (ROWS, LAGS * BLK)
    tiles = (QUAD, MINE, TROW, TCOL)
    block = pltpu.VMEM((NBLK, BLK, WIDE), BF16)
    n = len(PIECES)
    return pl.pallas_call(
        kernel,
        out_shape=jax.ShapeDtypeStruct((SLOTS, ROWS, LAGS * BLK), F32),
        in_specs=[hbm, hbm, smem, smem, smem],
        out_specs=vmem,
        scratch_shapes=[
            pltpu.VMEM((BLK, 2 * F), BF16),
            pltpu.VMEM((2, BANDS, LAGS, WIDE), F32),
            block, block, block, block,
            pltpu.VMEM((2, LAGS * BLK, WIDE), BF16),
            pltpu.VMEM((MINE, BLK, LAGS * BLK), F32),
            pltpu.VMEM((MINE, NY, *side), BF16),
            pltpu.VMEM((NY, MINE, *side), BF16),
            pltpu.VMEM((NY, MINE, *side), BF16),
            pltpu.VMEM((MINE, *side), BF16),
            pltpu.VMEM((MINE, *side), BF16),
            pltpu.VMEM((MINE, *side), BF16),
            pltpu.VMEM((QUAD, *tiles), F32),
            pltpu.VMEM((QUAD, *tiles), BF16),
            pltpu.VMEM((QUAD - 1, *tiles), BF16),
            pltpu.VMEM(tiles, F32),
            pltpu.VMEM(tiles, BF16),
            pltpu.VMEM((QUAD - 1, *tiles[1:]), BF16),
            pltpu.VMEM((MINE + 1, TROW, TCOL), BF16),
            pltpu.VMEM((NBLK, TROW, TCOL), BF16),
            pltpu.VMEM((NBLK, TROW, TCOL), BF16),
            pltpu.SMEM((NBLK,), jnp.int32),
            dma((BANDS + 2,)),
            dma((BANDS,)), dma((BANDS, 5)),
            dma((BANDS, 2)), dma((BANDS, 5, 2)),
            dma((BANDS, 3)), dma((BANDS, 3)),
            dma((n, NY)), dma((n, NY)),
            dma((n, 3)), dma((n, 3)),
            dma((n, QUAD - 1)), dma((n, QUAD - 1)),
            dma((n, QUAD - 1)), dma((n, QUAD - 1)),
            dma, dma,
        ],
        compiler_params=pltpu.CompilerParams(
            collective_id=0, has_side_effects=True, vmem_limit_bytes=58 << 20
        ),
        name="stack",
    )(spectra, phases, table, ranks, counts)


def phase_tables():
    freq = np.arange(F, dtype=np.int32).reshape(NZ, BANDS, 1, BAND)
    lag = np.arange(LAGS, dtype=np.int32)[:, None] - LAGS // 2
    phase = np.mod(lag * freq, 2 * F)
    angle = np.float32(np.pi) * phase.astype(np.float32) / np.float32(F)
    c, s = np.cos(angle), np.sin(angle)
    return np.stack([np.concatenate([c, c], -1), np.concatenate([s, -s], -1)], axis=1)


def plans(pairs, x):
    places = jnp.arange(NPAIRS, dtype=jnp.int32)
    keys = pairs[:, 2] * NPAIRS + places
    asked = jnp.concatenate([keys, jnp.arange(NBLK + 1, dtype=jnp.int32) * NPAIRS])
    ranks = jnp.sum((keys[None, :] < asked[:, None]).astype(jnp.int32), axis=1)
    wanted = places[:MINE] * NX + x
    pick = (ranks[None, :NPAIRS] == wanted[:, None]).astype(jnp.int32)
    blocks = pairs.T[:2]
    blocks = blocks % NX * NZ + blocks // NX
    return jnp.sum(pick[None] * blocks[:, None, :], axis=2), ranks


def per_device(spectra, block_counts, pairs):
    table, ranks = plans(pairs, lax.axis_index("chan") % NX)
    return call_kernel(spectra, jnp.asarray(phase_tables()), table, ranks, block_counts)


def solution(mesh):
    placed = (P("tm", "chan", None), P(), P())
    return jax.shard_map(
        per_device, mesh=mesh, in_specs=placed, out_specs=P("chan", "tm", None), check_vma=False
    )
```

```python
import jax
import jax.numpy as jnp
import numpy as np
from jax import lax
from jax.experimental import pallas as pl
from jax.experimental.pallas import tpu as pltpu
from jax.sharding import PartitionSpec as P

F = 4096
BAND = 64
BLK = 128
LAGS = 8
SLOTS = 3
NBLK = 64
NPAIRS = 96
SCALE = 1.0 / 256.0
MESH = pl.DeviceIdType.MESH
BF16 = jnp.bfloat16
F32 = jnp.float32

NZ, NX, NY = 16, 4, 4
BANDS = F // BAND // NZ
WIDE = 2 * BAND
MINE = NPAIRS // NX
PIECES = (2, 2, 3, 3, 3, 3, 4, 4)
FIRST = tuple(sum(PIECES[:b]) for b in range(len(PIECES)))
QUAD = 4
ROWS = 16
TROW, TCOL = 8, 128
TALL, FLAT = ROWS // TROW, LAGS * BLK // TCOL

GROUPS = ((0, 1, 15, 2), (14, 3, 13, 4), (12, 5, 11, 6), (10, 7, 9, 8))
LAST = GROUPS[:3] + ((10, 7), (9, 8))


def groups_of(q):
    return LAST if q == BANDS - 1 else GROUPS


def place():
    tm, chan = lax.axis_index("tm"), lax.axis_index("chan")
    return tm // 2, tm % 2, chan // NX, chan % NX


def remote(src, dst, send, recv, where):
    return pltpu.make_async_remote_copy(
        src_ref=src, dst_ref=dst, send_sem=send, recv_sem=recv, device_id=where, device_id_type=MESH
    )


def bytes_of(ref, sem):
    pltpu.make_async_copy(ref, ref, sem).wait()


def kernel(
    spectra, phases, table, ranks, counts, out,
    spec, trig, held0, held1, held2, held3, moved, acc, part, mine, other, h, u, v,
    sums, sent1, got1, sum2, sent2, got2, final, give, got, spot,
    local, zsend, zrecv, xsend, xrecv, fsend, frecv,
    csend, crecv, ysend, yrecv, send1, recv1, send2, recv2, gsend, grecv,
):
    y, c, z, x = place()
    chan = lax.axis_index("chan")
    owners = NZ * NX
    xl, xr = (x + NX - 1) % NX, (x + 1) % NX
    right, left = {"chan": z * NX + xr}, {"chan": z * NX + xl}
    core = {"tm": y * 2 + 1 - c}
    up, down = {"tm": (y + 1) % NY * 2 + c}, {"tm": (y + NY - 1) % NY * 2 + c}
    opposite = {"chan": z * NX + (x + 2) % NX}
    held = (held0, held1, held2, held3)

    def slot(xs, zs):
        return xs * NZ + zs

    def slots(xs, n):
        return pl.ds(xs * NZ, n)

    load = pltpu.make_async_copy(spectra.at[0], spec, local.at[BANDS])
    load.start()
    load_trig = pltpu.make_async_copy(phases.at[z], trig, local.at[BANDS + 1])
    load_trig.start()

    barrier = pltpu.get_barrier_semaphore()
    for where in (core, up, down):
        pl.semaphore_signal(barrier, inc=1, device_id=where, device_id_type=MESH)

    for where in [right, left, opposite] + [{"chan": (z + d) % NZ * NX + x} for d in range(1, NZ)]:
        pl.semaphore_signal(barrier, inc=1, device_id=where, device_id_type=MESH)
    load.wait()
    load_trig.wait()
    alive = (lax.broadcasted_iota(jnp.int32, (BLK, WIDE), 0) < counts[chan]).astype(F32)

    def whiten(q):
        def one(zt, carry):
            cols = pl.ds(pl.multiple_of((zt * BANDS + q) * WIDE, WIDE), WIDE)
            t = spec[:, cols].astype(F32)
            power = jnp.sum(t * t, axis=-1, keepdims=True) * (1.0 / BAND)
            spec[:, cols] = (t * lax.rsqrt(power + 1e-06) * alive).astype(BF16)
            return carry

        lax.fori_loop(0, NZ, one, 0)

    whiten(0)
    pl.semaphore_wait(barrier, NZ - 1 + 6)

    def columns(zt, q):
        return spec.at[:, pl.ds(pl.multiple_of((zt * BANDS + q) * WIDE, WIDE), WIDE)]

    def own(q):
        return pltpu.make_async_copy(columns(z, q), held[q].at[slot(x, z)], local.at[q])

    def zsends(q):
        for j, group in enumerate(groups_of(q)):
            for d in group:
                if d:
                    zt = (z + d) % NZ
                    remote(
                        columns(zt, q), held[q].at[slot(x, z)], zsend.at[q], zrecv.at[q, j],
                        {"chan": zt * NX + x},
                    ).start()

    def zwait(q, j):
        n = len(groups_of(q)[j])
        if j == 0:
            own(q).wait()
            n -= 1
        bytes_of(held[q].at[slots(x, n)], zrecv.at[q, j])

    def direct(q, j):
        return q == BANDS - 1 and j >= 3

    def xstart(q, j):
        for d in groups_of(q)[j]:
            blk = held[q].at[slot(x, (z + NZ - d) % NZ)]
            remote(blk, blk, xsend.at[q, 0], xrecv.at[q, j, 0], right).start()
            remote(blk, blk, xsend.at[q, 1], xrecv.at[q, j, 1], left).start()
            if direct(q, j):
                remote(blk, blk, fsend.at[q, 2], frecv.at[q, 2], opposite).start()

    def forward(q, j):
        group = groups_of(q)[j]
        n = len(group)
        for side, (xs, where) in enumerate(((xl, right), (xr, left))):
            bytes_of(held[q].at[slots(xs, n)], xrecv.at[q, j, side])
            if not direct(q, j):
                for d in group[side * n // 2 : (side + 1) * n // 2]:
                    blk = held[q].at[slot(xs, (z + NZ - d) % NZ)]
                    remote(blk, blk, fsend.at[q, side], frecv.at[q, side], where).start()

    def passed(q):
        return 6 if q == BANDS - 1 else 8

    def fwait(q):
        for side in range(2):
            bytes_of(held[q].at[slots(x, passed(q))], frecv.at[q, side])
        if q == BANDS - 1:
            bytes_of(held[q].at[slots(x, 4)], frecv.at[q, 2])

    def pair(q, p, slot):
        t = held[q][table[1, p]].astype(F32)
        w = pltpu.roll(t, BAND, 1)
        for m in range(LAGS):
            moved[slot, m * BLK : (m + 1) * BLK] = (
                t * trig[0, q, m : m + 1, :] + w * trig[1, q, m : m + 1, :]
            ).astype(BF16)
        corr = lax.dot_general(
            held[q][table[0, p]], moved[slot], (((1,), (1,)), ((), ())),
            preferred_element_type=F32,
        )
        if q == 0:
            acc[p] = corr
        elif q < BANDS - 1:
            acc[p] = acc[p] + corr
        else:
            acc[p] = (acc[p] + corr) * SCALE
            for k in range(NY):
                part[p, k] = acc[p, rows(k, 1 - c)].astype(BF16)

    def rows(k, core_):
        return pl.ds(pl.multiple_of((k * 2 + core_) * ROWS, ROWS), ROWS)

    def some_pairs(q, first, count):
        def one(i, carry):
            for slot in range(2):
                pair(q, first + i * 2 + slot, slot)
            return carry

        lax.fori_loop(0, count // 2, one, 0)

    for q in range(BANDS):
        own(q).start()
        zsends(q)
        if q < BANDS - 1:
            whiten(q + 1)

    def find(o, carry):
        first = ranks[NPAIRS + o]
        count = ranks[NPAIRS + o + 1] - first
        skip = (x + 4 * NPAIRS - first) % NX
        spot[o] = jnp.where(skip < count, (first + skip) // NX, MINE)
        return carry

    lax.fori_loop(0, owners, find, 0)

    third = MINE // 3
    prev = None
    for q in range(BANDS):
        for j in range(len(groups_of(q))):
            zwait(q, j)
            xstart(q, j)
            if prev is not None:
                forward(*prev)
            prev = (q, j)
            if q and j == 1:
                fwait(q - 1)
                some_pairs(q - 1, 0, third)
            elif q and j == 2:
                some_pairs(q - 1, third, 2 * third)
    end = BANDS - 1
    forward(*prev)
    fwait(end)

    y2, yp, ym = (y + 2) % NY, (y + 1) % NY, (y + NY - 1) % NY
    turn = [y2, yp, ym, y]

    def piece(b):
        return pl.ds(FIRST[b], PIECES[b])

    def swap(b, i):
        k = turn[i]
        return remote(
            part.at[piece(b), k], other.at[k, piece(b)], csend.at[b, i], crecv.at[b, i], core
        )

    def swaps(b):
        for i in range(NY):
            swap(b, i).start()

    def add_swap(b, i):
        swap(b, i).wait_recv()
        k = turn[i]

        def one(p, carry):
            mine[k, p] = (acc[p, rows(k, c)] + other[k, p].astype(F32)).astype(BF16)
            return carry

        lax.fori_loop(FIRST[b], FIRST[b] + PIECES[b], one, 0)

    nxt, bck = [yp, ym], [ym, yp]
    ahead, behind = [up, down], [down, up]

    def far(b):
        return remote(mine.at[y2, piece(b)], h.at[piece(b)], ysend.at[b, 0], yrecv.at[b, 0], ahead[b % 2])

    def raw(b):
        return remote(
            mine.at[bck[b % 2], piece(b)], v.at[piece(b)], ysend.at[b, 1], yrecv.at[b, 1], behind[b % 2]
        )

    def near(b):
        return remote(
            mine.at[nxt[b % 2], piece(b)], u.at[piece(b)], ysend.at[b, 2], yrecv.at[b, 2], ahead[b % 2]
        )

    def to_far(b):
        add_swap(b, 0)
        far(b).start()
        back = 2 - b % 2
        add_swap(b, back)
        raw(b).start()
        add_swap(b, 3 - back)
        add_swap(b, 3)

    def to_near(b):
        far(b).wait_recv()
        k = nxt[b % 2]

        def one(p, carry):
            mine[k, p] = (mine[k, p].astype(F32) + h[p].astype(F32)).astype(BF16)
            return carry

        lax.fori_loop(FIRST[b], FIRST[b] + PIECES[b], one, 0)
        near(b).start()

    four, at = z // QUAD, z % QUAD

    def near_z(b, k):
        m = (at + k) % QUAD
        return remote(
            sent1.at[m, :, piece(b)], got1.at[k - 1, :, piece(b)], send1.at[b, k - 1],
            recv1.at[b, k - 1], {"chan": (four * QUAD + m) * NX + x},
        )

    def far_z(b, k):
        f = (four + k) % QUAD
        return remote(
            sent2.at[f, piece(b)], got2.at[k - 1, piece(b)], send2.at[b, k - 1],
            recv2.at[b, k - 1], {"chan": (f * QUAD + at) * NX + x},
        )

    def to_sums(b):
        raw(b).wait_recv()
        near(b).wait_recv()

        def one(p, carry):
            t = mine[y, p].astype(F32) + u[p].astype(F32) + v[p].astype(F32)
            for i in range(NZ):
                r, l = i // FLAT, i % FLAT
                tile = t[r * TROW : (r + 1) * TROW, l * TCOL : (l + 1) * TCOL]
                sums[i % QUAD, i // QUAD, p] = tile
                sent1[i % QUAD, i // QUAD, p] = tile.astype(BF16)
            return carry

        lax.fori_loop(FIRST[b], FIRST[b] + PIECES[b], one, 0)
        for k in range(1, QUAD):
            near_z(b, k).start()

    def to_far_z(b):
        for k in range(1, QUAD):
            near_z(b, k).wait_recv()
        for f in range(QUAD):
            t = sums[at, f, piece(b)]
            for k in range(QUAD - 1):
                t = t + got1[k, f, piece(b)].astype(F32)
            sum2[f, piece(b)] = t
            sent2[f, piece(b)] = t.astype(BF16)
        for k in range(1, QUAD):
            far_z(b, k).start()

    def to_final(b):
        t = sum2[four, piece(b)]
        for k in range(1, QUAD):
            far_z(b, k).wait_recv()
            t = t + got2[k - 1, piece(b)].astype(F32)
        final[piece(b)] = t.astype(final.dtype)

    def both(stage, *couples):
        for g in couples:
            stage(2 * g)
            stage(2 * g + 1)

    def compute(b):
        some_pairs(end, FIRST[b], PIECES[b] + PIECES[b + 1])
        swaps(b)
        swaps(b + 1)

    couples = len(PIECES) // 2
    compute(0)
    compute(2)
    both(to_far, 0)
    for g in range(2, couples):
        compute(2 * g)
    for g in range(couples):
        both(to_near, g)
        if g + 1 < couples:
            both(to_far, g + 1)
        if g:
            both(to_far_z, g - 1)
        both(to_sums, g)
    both(to_far_z, couples - 1)
    both(to_final, *range(couples))
    final[MINE] = jnp.zeros((TROW, TCOL), final.dtype)

    def fill(o):
        give[o] = final[spot[o]]

    def deliver(k, carry):
        zt = (z + 8 + (1 - 2 * (k % 2)) * ((k + 1) // 2)) % NZ
        for xt in range(NX):
            o = zt * NX + xt
            fill(o)
            remote(give.at[o], got.at[chan], gsend, grecv, {"chan": o}).start()
        return carry

    lax.fori_loop(0, NZ - 1, deliver, 0)
    for k in range(1, NX):
        o = z * NX + (x + k) % NX
        fill(o)
        remote(give.at[o], got.at[chan], gsend, grecv, {"chan": o}).start()
    fill(chan)
    got[chan] = give[chan]
    many = pl.ds(0, owners - 1)
    bytes_of(got.at[many], grecv)

    first = ranks[NPAIRS + chan]
    count = ranks[NPAIRS + chan + 1] - first
    for k in range(SLOTS):
        group = (first + k) % NX
        for r in range(TALL):
            for l in range(FLAT):
                t = got[(r * FLAT + l) * NX + group].astype(F32)
                out[k, r * TROW : (r + 1) * TROW, l * TCOL : (l + 1) * TCOL] = jnp.where(
                    k < count, t, 0.0
                ).astype(BF16)

    bytes_of(give.at[many], gsend)
    for q in range(BANDS):
        bytes_of(held[q].at[slots(x, NZ - 1)], zsend.at[q])
        for side in range(2):
            bytes_of(held[q].at[slots(x, NZ)], xsend.at[q, side])
            bytes_of(held[q].at[slots(x, passed(q))], fsend.at[q, side])
        if q == BANDS - 1:
            bytes_of(held[q].at[slots(x, 4)], fsend.at[q, 2])
    for b in range(len(PIECES)):
        for i in range(NY):
            swap(b, i).wait_send()
        far(b).wait_send()
        raw(b).wait_send()
        near(b).wait_send()
        for k in range(1, QUAD):
            near_z(b, k).wait_send()
            far_z(b, k).wait_send()


def call_kernel(spectra, phases, table, ranks, counts):
    smem = pl.BlockSpec(memory_space=pltpu.SMEM)
    vmem = pl.BlockSpec(memory_space=pltpu.VMEM)
    hbm = pl.BlockSpec(memory_space=pl.ANY)
    dma = pltpu.SemaphoreType.DMA
    side = (ROWS, LAGS * BLK)
    tiles = (QUAD, MINE, TROW, TCOL)
    block = pltpu.VMEM((NBLK, BLK, WIDE), BF16)
    n = len(PIECES)
    return pl.pallas_call(
        kernel,
        out_shape=jax.ShapeDtypeStruct((SLOTS, ROWS, LAGS * BLK), BF16),
        in_specs=[hbm, hbm, smem, smem, smem],
        out_specs=vmem,
        scratch_shapes=[
            pltpu.VMEM((BLK, 2 * F), BF16),
            pltpu.VMEM((2, BANDS, LAGS, WIDE), F32),
            block, block, block, block,
            pltpu.VMEM((2, LAGS * BLK, WIDE), BF16),
            pltpu.VMEM((MINE, BLK, LAGS * BLK), F32),
            pltpu.VMEM((MINE, NY, *side), BF16),
            pltpu.VMEM((NY, MINE, *side), BF16),
            pltpu.VMEM((NY, MINE, *side), BF16),
            pltpu.VMEM((MINE, *side), BF16),
            pltpu.VMEM((MINE, *side), BF16),
            pltpu.VMEM((MINE, *side), BF16),
            pltpu.VMEM((QUAD, *tiles), F32),
            pltpu.VMEM((QUAD, *tiles), BF16),
            pltpu.VMEM((QUAD - 1, *tiles), BF16),
            pltpu.VMEM(tiles, F32),
            pltpu.VMEM(tiles, BF16),
            pltpu.VMEM((QUAD - 1, *tiles[1:]), BF16),
            pltpu.VMEM((MINE + 1, TROW, TCOL), BF16),
            pltpu.VMEM((NBLK, TROW, TCOL), BF16),
            pltpu.VMEM((NBLK, TROW, TCOL), BF16),
            pltpu.SMEM((NBLK,), jnp.int32),
            dma((BANDS + 2,)),
            dma((BANDS,)), dma((BANDS, 5)),
            dma((BANDS, 2)), dma((BANDS, 5, 2)),
            dma((BANDS, 3)), dma((BANDS, 3)),
            dma((n, NY)), dma((n, NY)),
            dma((n, 3)), dma((n, 3)),
            dma((n, QUAD - 1)), dma((n, QUAD - 1)),
            dma((n, QUAD - 1)), dma((n, QUAD - 1)),
            dma, dma,
        ],
        compiler_params=pltpu.CompilerParams(
            collective_id=0, has_side_effects=True, vmem_limit_bytes=58 << 20
        ),
        name="stack",
    )(spectra, phases, table, ranks, counts)


def phase_tables():
    freq = np.arange(F, dtype=np.int32).reshape(NZ, BANDS, 1, BAND)
    lag = np.arange(LAGS, dtype=np.int32)[:, None] - LAGS // 2
    phase = np.mod(lag * freq, 2 * F)
    angle = np.float32(np.pi) * phase.astype(np.float32) / np.float32(F)
    c, s = np.cos(angle), np.sin(angle)
    return np.stack([np.concatenate([c, c], -1), np.concatenate([s, -s], -1)], axis=1)


def plans(pairs, x):
    places = jnp.arange(NPAIRS, dtype=jnp.int32)
    keys = pairs[:, 2] * NPAIRS + places
    asked = jnp.concatenate([keys, jnp.arange(NBLK + 1, dtype=jnp.int32) * NPAIRS])
    ranks = jnp.sum((keys[None, :] < asked[:, None]).astype(jnp.int32), axis=1)
    wanted = places[:MINE] * NX + x
    pick = (ranks[None, :NPAIRS] == wanted[:, None]).astype(jnp.int32)
    blocks = pairs.T[:2]
    blocks = blocks % NX * NZ + blocks // NX
    return jnp.sum(pick[None] * blocks[:, None, :], axis=2), ranks


def per_device(spectra, block_counts, pairs):
    table, ranks = plans(pairs, lax.axis_index("chan") % NX)
    stacks = call_kernel(spectra, jnp.asarray(phase_tables()), table, ranks, block_counts)
    return stacks.astype(F32)


def solution(mesh):
    placed = (P("tm", "chan", None), P(), P())
    return jax.shard_map(
        per_device, mesh=mesh, in_specs=placed, out_specs=P("chan", "tm", None), check_vma=False
    )
```
